32 devices in a mesh: scene: 2 (over y), tok: 4 (over z), col: 2 (over x), rep: 2 (over core).
Axes of the slice: x: 2, y: 2, z: 4, core: 2. Of those that a mesh axis runs over, the one named last changes fastest.
Arguments:
- tokens: float32 [8192, 512], P(('scene', 'tok'), ('col', 'rep')), parts along dimension 0
- w_qkv: float32 [2, 3, 512, 512], P(None, None, None, ('col', 'rep'))
- w_out: float32 [2, 512, 512], P(None, ('col', 'rep')), may hold values from -0.25 to 0.25
- w_up: float32 [2, 512, 2048], P(None, None, ('col', 'rep')), may hold values from -0.25 to 0.25
- w_down: float32 [2, 2048, 512], P(None, ('col', 'rep')), may hold values from -0.125 to 0.125
- attn_gain: float32 [2, 512], replicated, may hold values from 0.1 to 1.9
- mlp_gain: float32 [2, 512], replicated, may hold values from 0.1 to 1.9
- dest_device: int32 [128], P(('scene', 'tok')), parts along dimension 0, may hold values from 0 to 3, as said below
- dest_slot: int32 [128], P(('scene', 'tok')), parts along dimension 0, may hold values from 0 to 15, as said below
- pillar: int32 [8192], P(('scene', 'tok')), parts along dimension 0, may hold values from -1 to 2047, as said below
- depth_weight: float32 [2, 3, 3, 512], replicated, may hold values from -2 to 2
- point_weight: float32 [2, 512, 1024], replicated, may hold values from -0.25 to 0.25
- raster_gain: float32 [2, 512], replicated, may hold values from 0.1 to 1.9
Outputs:
- raster: float32 [128, 32, 512], P(('scene', 'tok', 'rep'), 'col'), parts along dimension 0
The draws below stay inside these ranges and needn't reach their ends.
There are 2 independent parts, one for each index of `scene`. The reference program is written for one: setup_inputs(seed, part) draws one part's arguments, and reference() takes and returns one part's arrays. A program takes and returns all parts, laid end to end along the dimension named above; an argument that names none is the same for every part. Nothing has to cross between parts.
Inputs may be any that keep to these rules, and one draw needn't show every extreme that they name: `dest_device`: together with dest_slot the blocks fill every index of tok's 16 slots exactly once. At most 5 blocks of one index of tok go to one index, and every index sends exactly 5 blocks to some index. `dest_slot`: the slot of the block among the 16 of its destination. The token at Hilbert position t has a cell in raster rows i * 16 to (i + 1) * 16 - 1 with i = t // 1024, or -1 if it has no pillar; several tokens may share a cell.
All inputs are finite; a program needn't handle non-finite values.
Results may differ from the reference program's by a relative error of at most 0.00012.
Values sent between devices are 32-bit elements; how exact they have to be, the bound alone decides.
A program may use at most 128 MiB of HBM per device.

```python
import jax
import jax.numpy as jnp
from jax import lax

D = 512
HEADS = 32
FF = 2048
PATCH = 1024
BLOCK = 64
TR = 16
TC = 16
HD = 16
TOK_DEV = 1024
TOKENS = 4096
BLK_DEV = 16
NB = 64
H = 64
W = 32
N_TOK = 4
N_COL = 2


def draw_tokens(key, part):
    first_key = jax.random.fold_in(jax.random.fold_in(key, 3), 0)
    values = jax.random.normal(first_key, (TOKENS, D), jnp.float32)
    return values


def draw_w_qkv(key, part):
    first_key = jax.random.fold_in(jax.random.fold_in(key, 5), 0)
    base = jax.random.normal(first_key, (2, 3, D, D), jnp.float32) * D ** (-0.5)
    return base


def route_tables(key):
    first_key, second_key, third_key, fourth_key = jax.random.split(jax.random.fold_in(key, 29), 4)
    owners = jax.random.permutation(first_key, N_TOK).astype(jnp.int32)
    spread = jax.random.permutation(second_key, BLK_DEV - 2).astype(jnp.int32)
    shifts = jnp.concatenate([jnp.zeros((2,), jnp.int32), 1 + spread % (N_TOK - 1)])

    def permute_single_block(subkey):
        return jax.random.permutation(subkey, BLK_DEV).astype(jnp.int32)
    order = jax.vmap(permute_single_block)(jax.random.split(third_key, N_TOK))
    arrival = jax.vmap(permute_single_block)(jax.random.split(fourth_key, N_TOK))
    source = jnp.arange(N_TOK, dtype=jnp.int32)[:, None]
    target = owners[(source + shifts[order]) % N_TOK]
    slots = arrival[target, order]
    return (target.reshape(-1).astype(jnp.int32), slots.reshape(-1).astype(jnp.int32))


def draw_dest_device(key, part):
    return route_tables(key)[0]


def draw_dest_slot(key, part):
    return route_tables(key)[1]


def draw_pillar(key, part):
    first_key, second_key, third_key = jax.random.split(jax.random.fold_in(key, 41), 3)
    full_width = TC * N_COL
    band = jnp.arange(TOKENS, dtype=jnp.int32) // TOK_DEV
    row_in = jax.random.randint(first_key, (TOKENS,), 0, TR, jnp.int32)
    col_in = jax.random.randint(second_key, (TOKENS,), 0, full_width, jnp.int32)
    present = jax.random.randint(third_key, (TOKENS,), 0, 8, jnp.int32) < 7
    return jnp.where(present, (band * TR + row_in) * full_width + col_in, -1).astype(jnp.int32)


def shard_levels(own_key, dims, pieces, low, high):
    gain = 1.0
    for axis_at, shards_of in pieces:
        draws = jax.random.uniform(jax.random.fold_in(jax.random.fold_in(own_key, 6), axis_at), (shards_of,), jnp.float32, low / len(pieces), high / len(pieces))
        gain = gain * jnp.repeat(jnp.exp(draws), dims[axis_at] // shards_of).reshape((-1,) + (1,) * (len(dims) - 1 - axis_at))
    return gain


def centred(rng, dims, deviation, limit, cuts=(), kind=jnp.bfloat16):
    gain = shard_levels(rng, dims, cuts, -0.22, 0.18) if cuts else 1.0
    array = jax.random.normal(rng, dims, jnp.float32) * deviation * gain
    return jnp.minimum(jnp.maximum(array, -limit), limit).astype(kind)


def setup_inputs(seed: int = 0, part: int = 0) -> dict:
    seeds = jax.random.split(jax.random.key(seed), 14)
    part_keys = jax.random.split(jax.random.fold_in(seeds[13], part), 14)
    tokens = draw_tokens(jax.random.fold_in(jax.random.fold_in(seeds[13], part), 71), part)
    w_qkv = draw_w_qkv(jax.random.fold_in(seeds[13], 71), part)
    w_out = centred(seeds[2], (2, D, D), D ** -0.5, 0.25, ((1, 4),), jnp.float32)
    w_up = centred(seeds[3], (2, D, FF), D ** -0.5, 0.25, ((2, 4),), jnp.float32)
    w_down = centred(seeds[4], (2, FF, D), FF ** -0.5, 0.125, ((1, 4),), jnp.float32)
    attn_gain = jnp.clip(1.0 + 0.18 * jax.random.normal(seeds[5], (2, D), jnp.float32), 0.1, 1.9)
    mlp_gain = jnp.clip(1.0 + 0.18 * jax.random.normal(seeds[6], (2, D), jnp.float32), 0.1, 1.9)
    dest_device = draw_dest_device(jax.random.fold_in(jax.random.fold_in(seeds[13], part), 71), part)
    dest_slot = draw_dest_slot(jax.random.fold_in(jax.random.fold_in(seeds[13], part), 71), part)
    pillar = draw_pillar(jax.random.fold_in(jax.random.fold_in(seeds[13], part), 71), part)
    depth_weight = centred(seeds[10], (2, 3, 3, D), 0.35, 2.0, (), jnp.float32)
    point_weight = centred(seeds[11], (2, D, 2 * D), D ** -0.5, 0.25, (), jnp.float32)
    raster_gain = jnp.clip(1.0 + 0.18 * jax.random.normal(seeds[12], (2, D), jnp.float32), 0.1, 1.9)
    return dict(tokens=tokens, w_qkv=w_qkv, w_out=w_out, w_up=w_up, w_down=w_down, attn_gain=attn_gain, mlp_gain=mlp_gain, dest_device=dest_device, dest_slot=dest_slot, pillar=pillar, depth_weight=depth_weight, point_weight=point_weight, raster_gain=raster_gain)


MATMUL_PRECISION = lax.Precision.HIGHEST
EPSILON = 1e-05

def layer_norm(values, gain_row):
    average = lax.optimization_barrier(jnp.mean(values, axis=-1, keepdims=True))
    centered = values - average
    variance = lax.optimization_barrier(jnp.mean(centered * centered, axis=-1, keepdims=True))
    return centered * lax.rsqrt(variance + EPSILON) * gain_row

def patch_attention(query_projection, key_proj, value_proj):
    scores = jnp.einsum('qhd,khd->hqk', query_projection, key_proj, precision=MATMUL_PRECISION) * HD ** (-0.5)
    scores = scores - lax.optimization_barrier(jnp.max(scores, axis=-1, keepdims=True))
    weights = jnp.exp(scores)
    weights = weights / lax.optimization_barrier(jnp.sum(weights, axis=-1, keepdims=True))
    return jnp.einsum('hqk,khd->qhd', weights, value_proj, precision=MATMUL_PRECISION)

def matmul(left, right):
    return jnp.dot(left, right, precision=MATMUL_PRECISION, preferred_element_type=jnp.float32)

def block_layer(stream, w_qkv, w_out, w_up, w_down, attn_gain, mlp_gain):
    row_count = stream.shape[0]
    normed = layer_norm(stream, attn_gain)
    shaped = tuple((matmul(normed, w_qkv[j]).reshape(row_count // PATCH, PATCH, HEADS, HD) for j in range(3)))

    def attend_patch(operands):
        return patch_attention(operands[0], operands[1], operands[2]).reshape(PATCH, D)
    attended = lax.map(attend_patch, shaped).reshape(row_count, D)
    stream = stream + matmul(attended, w_out)
    normed = layer_norm(stream, mlp_gain)
    hidden = jax.nn.gelu(matmul(normed, w_up), approximate=False)
    return stream + matmul(hidden, w_down)

def raster_layer(raster_grid, depth_weight, point_weight, gain_row):
    row_count, col_count, count_of_channels = raster_grid.shape
    normed = raster_grid * lax.rsqrt(lax.optimization_barrier(jnp.mean(raster_grid * raster_grid, axis=-1, keepdims=True)) + EPSILON) * gain_row
    padded = jnp.pad(normed, ((1, 1), (1, 1), (0, 0)))
    mixed_cells = jnp.zeros_like(raster_grid)
    for row_tap in range(3):
        for col_tap in range(3):
            mixed_cells = mixed_cells + padded[row_tap:row_tap + row_count, col_tap:col_tap + col_count] * depth_weight[row_tap, col_tap]
    combined = matmul(mixed_cells.reshape(row_count * col_count, count_of_channels), point_weight)
    combined = combined.reshape(row_count, col_count, 2 * count_of_channels)
    return raster_grid + combined[..., :count_of_channels] * jax.nn.sigmoid(combined[..., count_of_channels:])

def reference(tokens, w_qkv, w_out, w_up, w_down, attn_gain, mlp_gain, dest_device, dest_slot, pillar, depth_weight, point_weight, raster_gain):
    stream = block_layer(tokens, w_qkv[0], w_out[0], w_up[0], w_down[0], attn_gain[0], mlp_gain[0])
    block_list = stream.reshape(NB, BLOCK, D)
    position = (dest_device * BLK_DEV + dest_slot).astype(jnp.int32)
    reordered_tokens = jnp.zeros_like(block_list).at[position].set(block_list).reshape(TOKENS, D)
    stream = block_layer(reordered_tokens, w_qkv[1], w_out[1], w_up[1], w_down[1], attn_gain[1], mlp_gain[1])
    cell_ids = jnp.where(pillar < 0, H * W, pillar).astype(jnp.int32)
    pooled = jax.ops.segment_sum(stream, cell_ids, num_segments=H * W + 1)[:H * W]
    raster_grid = pooled.reshape(H, W, D)
    for layer_index in range(2):
        raster_grid = raster_layer(raster_grid, depth_weight[layer_index], point_weight[layer_index], raster_gain[layer_index])
    return raster_grid
```

```python
import functools
import math

import jax
import jax.numpy as jnp
from jax import lax
from jax.experimental import pallas as pl
from jax.experimental.pallas import tpu as pltpu
from jax.sharding import PartitionSpec as P

PATCH = 1024
TR = 16
TC = 16
HD = 16


MATMUL_PRECISION = lax.Precision.HIGH
EPSILON = 1e-05


def layer_norm(values, gain_row):
    average = jnp.mean(values, axis=-1, keepdims=True)
    centered = values - average
    variance = jnp.mean(centered * centered, axis=-1, keepdims=True)
    return centered * lax.rsqrt(variance + EPSILON) * gain_row


def split(values):
    high = values.astype(jnp.bfloat16)
    return high, (values - high.astype(jnp.float32)).astype(jnp.bfloat16)


def bdot(left, right, dims=(((1,), (0,)), ((), ()))):
    return lax.dot_general(left, right, dims, preferred_element_type=jnp.float32)


def dot3(left, right):
    lh, ll = left
    rh, rl = right
    return bdot(lh, rh) + bdot(lh, rl) + bdot(ll, rh)


def attention_kernel(x_ref, gain_ref, w_ref, out_ref, q_s, k_s, v_s):
    cols = w_ref.shape[-1]
    heads = cols // HD
    rows = x_ref.shape[0]
    chunk = 256
    lanes = q_s.shape[-1]

    r = lax.broadcasted_iota(jnp.int32, (cols, lanes), 0)
    c = lax.broadcasted_iota(jnp.int32, (cols, lanes), 1)
    lane = lax.broadcasted_iota(jnp.int32, (1, cols), 1)
    w = [split(w_ref[j]) for j in range(3)]
    for i in range(rows // chunk):
        at = pl.ds(i * chunk, chunk)
        normed = split(layer_norm(x_ref[at, :], gain_ref[...]))
        qh, ql = split(dot3(normed, w[0]) * (HD ** (-0.5) * math.log2(math.e)))
        kh, kl = split(dot3(normed, w[1]))
        vh, vl = split(dot3(normed, w[2]))
        for h in range(heads):
            part = c // HD
            inside = (r // HD == h) & (r % HD == c % HD)
            first = (inside & ((part == 0) | (part == 1))).astype(jnp.bfloat16)
            third = (inside & (part == 2)).astype(jnp.bfloat16)
            outer = (inside & ((part == 0) | (part == 2))).astype(jnp.bfloat16)
            middle = (inside & (part == 1)).astype(jnp.bfloat16)
            q_s[h, at, :] = (bdot(qh, first) + bdot(ql, third)).astype(jnp.bfloat16)
            k_s[h, at, :] = (bdot(kh, outer) + bdot(kl, middle)).astype(jnp.bfloat16)
            own = lane // HD == h
            v_s[h, at, :cols] = jnp.where(own, vh.astype(jnp.float32), 0.0).astype(jnp.bfloat16)
            v_s[h, at, cols:] = jnp.where(own, vl.astype(jnp.float32), 1.0).astype(jnp.bfloat16)

    out_ref[...] = jnp.zeros_like(out_ref)
    for i in range(rows // chunk):
        at = pl.ds(i * chunk, chunk)

        def one_head(h, carry):
            scores = bdot(q_s[h, at, :], k_s[h], (((1,), (1,)), ((), ())))
            weights = jnp.exp2(scores - jnp.max(scores, axis=-1, keepdims=True))
            wh, wl = split(weights)
            sums = bdot(wh, v_s[h]) + bdot(wl, v_s[h])
            top, low = sums[:, :cols], sums[:, cols:]
            own = lane // HD == h
            total = jnp.max(jnp.where(own, 0.0, low), axis=-1, keepdims=True)
            out_ref[at, :] += jnp.where(own, (top + low) / total, 0.0)
            return carry

        lax.fori_loop(0, heads, one_head, 0, unroll=2)


def attend(stream, gain_row, weights):
    rows, width = stream.shape
    cols = weights.shape[-1]
    heads = cols // HD
    lanes = max(128, 3 * HD)
    return pl.pallas_call(
        attention_kernel,
        grid=(rows // PATCH,),
        in_specs=[
            pl.BlockSpec((PATCH, width), lambda i: (i, 0)),
            pl.BlockSpec((1, width), lambda i: (0, 0)),
            pl.BlockSpec(weights.shape, lambda i: (0, 0, 0)),
        ],
        out_specs=pl.BlockSpec((PATCH, cols), lambda i: (i, 0)),
        out_shape=jax.ShapeDtypeStruct((rows, cols), jnp.float32),
        scratch_shapes=[
            pltpu.VMEM((heads, PATCH, lanes), jnp.bfloat16),
            pltpu.VMEM((heads, PATCH, lanes), jnp.bfloat16),
            pltpu.VMEM((heads, PATCH, 2 * cols), jnp.bfloat16),
        ],
        compiler_params=pltpu.CompilerParams(vmem_limit_bytes=48 * 1024 * 1024),
        name="attend",
    )(stream, gain_row[None, :], weights)


def matmul(left, right):
    return jnp.dot(left, right, precision=MATMUL_PRECISION, preferred_element_type=jnp.float32)


def widen(slice_cols):
    return lax.all_gather(slice_cols, ("col", "rep"), axis=1, tiled=True)


def attention_layer(stream, layer, w_qkv, w_out, attn_gain):
    attended = attend(stream, attn_gain[layer], w_qkv[layer])
    return stream + lax.psum(matmul(attended, w_out[layer]), ("col", "rep"))


def mlp_partial(stream, layer, w_up, w_down, mlp_gain):
    normed = layer_norm(stream, mlp_gain[layer])
    hidden = jax.nn.gelu(matmul(normed, w_up[layer]), approximate=False)
    return matmul(hidden, w_down[layer])


def send_blocks(block_list, dest_device, dest_slot):
    block_count, rows_per_block, feature_width = block_list.shape
    peers = lax.axis_size("tok")
    capacity = max(2, (block_count + peers - 4) // (peers - 1))
    order_index = jnp.arange(block_count, dtype=jnp.int32)
    earlier = (dest_device[:, None] == dest_device[None, :]) & (
        order_index[None, :] < order_index[:, None]
    )
    prior_count = jnp.sum(earlier.astype(jnp.int32), axis=1)
    slot_key = dest_device * capacity + prior_count
    select_entries = (
        jnp.arange(peers * capacity, dtype=jnp.int32)[:, None] == slot_key[None, :]
    ).astype(jnp.float32)
    outgoing = jnp.einsum(
        "jb,brf->jrf", select_entries, block_list, precision=MATMUL_PRECISION
    ).reshape(peers, capacity, rows_per_block, feature_width)
    slot_codes = matmul(select_entries, (dest_slot + 1).astype(jnp.float32)).reshape(
        peers, capacity
    )
    incoming, arrived = (
        lax.all_to_all(outgoing, "tok", split_axis=0, concat_axis=0, tiled=True),
        lax.all_to_all(slot_codes, "tok", split_axis=0, concat_axis=0, tiled=True),
    )
    wanted = (order_index + 1).astype(jnp.float32)
    placing = (wanted[:, None] == arrived.reshape(-1)[None, :]).astype(jnp.float32)
    flat_incoming = incoming.reshape(peers * capacity, rows_per_block, feature_width)
    return jnp.einsum("sj,jrf->srf", placing, flat_incoming, precision=MATMUL_PRECISION)


def raster_cells(extended, depth_weight, point_weight, gain_row):
    row_count = extended.shape[0] - 2
    col_count = extended.shape[1] - 2
    channels = extended.shape[2]
    normed = (
        extended
        * lax.rsqrt(jnp.mean(extended * extended, axis=-1, keepdims=True) + EPSILON)
        * gain_row
    )
    mixed = jnp.zeros((row_count, col_count, channels), jnp.float32)
    for a in range(3):
        for b in range(3):
            mixed = mixed + normed[a : a + row_count, b : b + col_count] * depth_weight[a, b]
    combined = matmul(mixed.reshape(row_count * col_count, channels), point_weight)
    combined = combined.reshape(row_count, col_count, 2 * channels)
    centre = extended[1:-1, 1:-1]
    return centre + combined[..., :channels] * jax.nn.sigmoid(combined[..., channels:])


HALO = 2


def extended_cells(tok, members, rep_rows, full_width):
    cols, reps = members
    tile = []
    for col in range(cols):
        for rep in range(reps):
            y = rep * rep_rows - HALO + jnp.arange(rep_rows + 2 * HALO, dtype=jnp.int32)[:, None]
            x = col * TC - HALO + jnp.arange(TC + 2 * HALO, dtype=jnp.int32)[None, :]
            good = (y >= 0) & (y < TR) & (x >= 0) & (x < full_width)
            tile.append(jnp.where(good, (tok * TR + y) * full_width + x, -2).reshape(-1))
    return jnp.concatenate(tile)


def pool(partial, pillar, cells):
    onehot = (cells[:, None] == pillar[None, :]).astype(jnp.float32)
    return matmul(onehot, partial)


def exchange_rows(tile, ntok, reps):
    count = ntok * reps
    rep = lax.axis_index("rep")
    forward = [(i, i + 1) for i in range(count - 1)]
    backward = [(i + 1, i) for i in range(count - 1)]
    above = lax.ppermute(tile[-2 * HALO : -HALO], ("tok", "rep"), forward)
    below = lax.ppermute(tile[HALO : 2 * HALO], ("tok", "rep"), backward)
    above = jnp.where(rep == 0, above, tile[:HALO])
    below = jnp.where(rep == reps - 1, below, tile[-HALO:])
    return jnp.concatenate([above, tile[HALO:-HALO], below], axis=0)


def on_device(
    tokens,
    w_qkv,
    w_out,
    w_up,
    w_down,
    attn_gain,
    mlp_gain,
    dest_device,
    dest_slot,
    pillar,
    depth_weight,
    point_weight,
    raster_gain,
):
    members = (lax.axis_size("col"), lax.axis_size("rep"))
    group = members[0] * members[1]
    ntok = lax.axis_size("tok")
    stream = widen(tokens)
    stream = attention_layer(stream, 0, w_qkv, w_out, attn_gain)
    partial = mlp_partial(stream, 0, w_up, w_down, mlp_gain)
    share = lax.psum_scatter(partial, ("col", "rep"), scatter_dimension=1, tiled=True)
    width = share.shape[1]
    share = share + lax.dynamic_slice_in_dim(
        stream, lax.axis_index(("col", "rep")) * width, width, 1
    )
    block_count = dest_device.shape[0]
    block_list = share.reshape(block_count, -1, width)
    stream = widen(send_blocks(block_list, dest_device, dest_slot).reshape(-1, width))
    stream = attention_layer(stream, 1, w_qkv, w_out, attn_gain)
    partial = mlp_partial(stream, 1, w_up, w_down, mlp_gain)

    rep_rows = TR // members[1]
    full_width = TC * members[0]
    cells = extended_cells(lax.axis_index("tok"), members, rep_rows, full_width)
    pooled = pool(partial + stream * (1.0 / group), pillar, cells)
    tile = lax.psum_scatter(pooled, ("col", "rep"), scatter_dimension=0, tiled=True)
    tile = tile.reshape(rep_rows + 2 * HALO, TC + 2 * HALO, -1)
    tile = exchange_rows(tile, ntok, members[1])
    first = raster_cells(tile, depth_weight[0], point_weight[0], raster_gain[0])
    y = lax.axis_index(("tok", "rep")) * rep_rows - 1 + jnp.arange(rep_rows + 2)[:, None, None]
    x = lax.axis_index("col") * TC - 1 + jnp.arange(TC + 2)[None, :, None]
    inside = (y >= 0) & (y < TR * ntok) & (x >= 0) & (x < full_width)
    first = jnp.where(inside, first, 0.0)
    return raster_cells(first, depth_weight[1], point_weight[1], raster_gain[1])


def solution(mesh):
    placed = (
        P(("scene", "tok"), ("col", "rep")),
        P(None, None, None, ("col", "rep")),
        P(None, ("col", "rep"), None),
        P(None, None, ("col", "rep")),
        P(None, ("col", "rep"), None),
        P(),
        P(),
        P(("scene", "tok")),
        P(("scene", "tok")),
        P(("scene", "tok")),
        P(),
        P(),
        P(),
    )
    return jax.shard_map(
        on_device,
        mesh=mesh,
        in_specs=placed,
        out_specs=P(("scene", "tok", "rep"), "col", None),
        check_vma=False,
    )
```

```python
import functools
import math

import jax
import jax.numpy as jnp
from jax import lax
from jax.experimental import pallas as pl
from jax.experimental.pallas import tpu as pltpu
from jax.sharding import PartitionSpec as P

PATCH = 1024
TR = 16
TC = 16
HD = 16


MATMUL_PRECISION = lax.Precision.HIGH
EPSILON = 1e-05


def layer_norm(values, gain_row):
    average = jnp.mean(values, axis=-1, keepdims=True)
    centered = values - average
    variance = jnp.mean(centered * centered, axis=-1, keepdims=True)
    return centered * lax.rsqrt(variance + EPSILON) * gain_row


def split(values):
    high = values.astype(jnp.bfloat16)
    return high, (values - high.astype(jnp.float32)).astype(jnp.bfloat16)


def bdot(left, right, dims=(((1,), (0,)), ((), ()))):
    return lax.dot_general(left, right, dims, preferred_element_type=jnp.float32)


def dot3(left, right):
    lh, ll = left
    rh, rl = right
    return bdot(lh, rh) + bdot(lh, rl) + bdot(ll, rh)


def attention_kernel(x_ref, gain_ref, w_ref, out_ref, q_s, k_s, v_s):
    cols = w_ref.shape[-1]
    heads = cols // HD
    rows = x_ref.shape[1]
    chunk = 256
    lanes = q_s.shape[-1]

    r = lax.broadcasted_iota(jnp.int32, (cols, lanes), 0)
    c = lax.broadcasted_iota(jnp.int32, (cols, lanes), 1)
    lane = lax.broadcasted_iota(jnp.int32, (1, cols), 1)
    w = [split(w_ref[j]) for j in range(3)]
    for i in range(rows // chunk):
        at = pl.ds(i * chunk, chunk)
        stream = jnp.concatenate([x_ref[j, at, :] for j in range(x_ref.shape[0])], axis=-1)
        normed = split(layer_norm(stream, gain_ref[...]))
        qh, ql = split(dot3(normed, w[0]) * (HD ** (-0.5) * math.log2(math.e)))
        kh, kl = split(dot3(normed, w[1]))
        vh, vl = split(dot3(normed, w[2]))
        for h in range(heads):
            part = c // HD
            inside = (r // HD == h) & (r % HD == c % HD)
            first = (inside & ((part == 0) | (part == 1))).astype(jnp.bfloat16)
            third = (inside & (part == 2)).astype(jnp.bfloat16)
            outer = (inside & ((part == 0) | (part == 2))).astype(jnp.bfloat16)
            middle = (inside & (part == 1)).astype(jnp.bfloat16)
            q_s[h, at, :] = (bdot(qh, first) + bdot(ql, third)).astype(jnp.bfloat16)
            k_s[h, at, :] = (bdot(kh, outer) + bdot(kl, middle)).astype(jnp.bfloat16)
            own = lane // HD == h
            v_s[h, at, :cols] = jnp.where(own, vh.astype(jnp.float32), 0.0).astype(jnp.bfloat16)
            v_s[h, at, cols:] = jnp.where(own, vl.astype(jnp.float32), 1.0).astype(jnp.bfloat16)

    out_ref[...] = jnp.zeros_like(out_ref)
    for i in range(rows // chunk):
        at = pl.ds(i * chunk, chunk)

        def one_head(h, carry):
            scores = bdot(q_s[h, at, :], k_s[h], (((1,), (1,)), ((), ())))
            weights = jnp.exp2(scores - jnp.max(scores, axis=-1, keepdims=True))
            wh, wl = split(weights)
            sums = bdot(wh, v_s[h]) + bdot(wl, v_s[h])
            top, low = sums[:, :cols], sums[:, cols:]
            own = lane // HD == h
            total = jnp.max(jnp.where(own, 0.0, low), axis=-1, keepdims=True)
            out_ref[at, :] += jnp.where(own, (top + low) / total, 0.0)
            return carry

        lax.fori_loop(0, heads, one_head, 0, unroll=2)


def attend(stream, gain_row, weights):
    slots, rows, width = stream.shape
    cols = weights.shape[-1]
    heads = cols // HD
    lanes = max(128, 3 * HD)
    return pl.pallas_call(
        attention_kernel,
        grid=(rows // PATCH,),
        in_specs=[
            pl.BlockSpec((slots, PATCH, width), lambda i: (0, i, 0)),
            pl.BlockSpec((1, slots * width), lambda i: (0, 0)),
            pl.BlockSpec(weights.shape, lambda i: (0, 0, 0)),
        ],
        out_specs=pl.BlockSpec((PATCH, cols), lambda i: (i, 0)),
        out_shape=jax.ShapeDtypeStruct((rows, cols), jnp.float32),
        scratch_shapes=[
            pltpu.VMEM((heads, PATCH, lanes), jnp.bfloat16),
            pltpu.VMEM((heads, PATCH, lanes), jnp.bfloat16),
            pltpu.VMEM((heads, PATCH, 2 * cols), jnp.bfloat16),
        ],
        compiler_params=pltpu.CompilerParams(vmem_limit_bytes=48 * 1024 * 1024),
        name="attend",
    )(stream, gain_row[None, :], weights)


def matmul(left, right):
    return jnp.dot(left, right, precision=MATMUL_PRECISION, preferred_element_type=jnp.float32)


VMEM_LIMIT = 56 * 1024 * 1024
MESH = pl.DeviceIdType.MESH


def position():
    cols, reps = lax.axis_size("col"), lax.axis_size("rep")
    return cols, reps, lax.axis_index("col"), lax.axis_index("rep")


def greet(devices):
    barrier = pltpu.get_barrier_semaphore()
    for device in devices:
        pl.semaphore_signal(barrier, inc=1, device_id=device, device_id_type=MESH)
    pl.semaphore_wait(barrier, len(devices))


def remote(src, dst, send, recv, device):
    return pltpu.make_async_remote_copy(
        src_ref=src, dst_ref=dst, send_sem=send, recv_sem=recv, device_id=device, device_id_type=MESH
    )


def chunks_of(rows):
    pieces = 4 if rows % 64 == 0 else (2 if rows % 16 == 0 else 1)
    return pieces, rows // pieces


def gather_kernel(x_ref, out_ref, xs, xr, fs, fr, ps, pr, local):
    cols, reps, c, r = position()
    rows = x_ref.shape[0]
    pieces, size = chunks_of(rows)
    me = c * reps + r
    mate = {"col": c, "rep": 1 - r}
    others = [{"col": lax.rem(c + d, cols), "rep": r} for d in range(1, cols)]
    greet([mate] + others)
    across, onward = [], []
    for k in range(pieces):
        at = pl.ds(k * size, size)
        for d in range(1, cols):
            copy = remote(
                x_ref.at[at], out_ref.at[me, at], xs.at[d - 1, k], xr.at[d - 1, k], others[d - 1]
            )
            copy.start()
            across.append(copy)
    share = remote(x_ref, out_ref.at[me], ps, pr, mate)
    share.start()
    keep = pltpu.make_async_copy(x_ref, out_ref.at[me], local)
    keep.start()
    for k in range(pieces):
        at = pl.ds(k * size, size)
        for d in range(1, cols):
            across[k * (cols - 1) + d - 1].wait_recv()
            slot = lax.rem(c + cols - d, cols) * reps + r
            copy = remote(
                out_ref.at[slot, at], out_ref.at[slot, at], fs.at[d - 1, k], fr.at[d - 1, k], mate
            )
            copy.start()
            onward.append(copy)
    for copy in across:
        copy.wait_send()
    share.wait()
    keep.wait()
    for copy in onward:
        copy.wait()


def gather(block, collective_id):
    cols, reps = lax.axis_size("col"), lax.axis_size("rep")
    if reps != 2 or cols < 2:
        return lax.all_gather(block, ("col", "rep"), axis=0)
    pieces, _ = chunks_of(block.shape[0])
    dma = pltpu.SemaphoreType.DMA
    return pl.pallas_call(
        gather_kernel,
        out_shape=jax.ShapeDtypeStruct((cols * reps,) + block.shape, block.dtype),
        in_specs=[pl.BlockSpec(memory_space=pltpu.VMEM)],
        out_specs=pl.BlockSpec(memory_space=pltpu.VMEM),
        scratch_shapes=[dma((cols - 1, pieces))] * 4 + [dma, dma, dma],
        compiler_params=pltpu.CompilerParams(
            collective_id=collective_id, has_side_effects=True, vmem_limit_bytes=VMEM_LIMIT
        ),
        name="gather",
    )(block)


def scatter_kernel(p_ref, out_ref, a_ref, s_ref, b_ref, a_s, a_r, b_s, b_r):
    cols, reps, c, r = position()
    rows = p_ref.shape[1]
    pieces, size = chunks_of(rows)
    mate = {"col": c, "rep": 1 - r}
    others = [{"col": lax.rem(c + d, cols), "rep": r} for d in range(1, cols)]
    greet([mate] + others)
    order = [(k, d) for k in range(pieces) for d in range(1, cols)]
    order += [(k, 0) for k in range(pieces)]
    near, far = {}, {}
    for k, d in order:
        at = pl.ds(k * size, size)
        slot = lax.rem(c + d, cols) * reps + 1 - r
        near[k, d] = remote(
            p_ref.at[slot, at], a_ref.at[d, at], a_s.at[d, k], a_r.at[d, k], mate
        )
        near[k, d].start()
    for k, d in order:
        at = pl.ds(k * size, size)
        slot = lax.rem(c + d, cols) * reps + r
        near[k, d].wait_recv()
        total = p_ref[slot, at] + a_ref[d, at]
        if d == 0:
            out_ref[at] = total
        else:
            s_ref[d - 1, at] = total
            far[k, d] = remote(
                s_ref.at[d - 1, at],
                b_ref.at[d - 1, at],
                b_s.at[d - 1, k],
                b_r.at[d - 1, k],
                others[d - 1],
            )
            far[k, d].start()
    for (k, d), copy in far.items():
        at = pl.ds(k * size, size)
        copy.wait_recv()
        out_ref[at] += b_ref[d - 1, at]
    for copy in list(near.values()) + list(far.values()):
        copy.wait_send()


def scatter(parts, collective_id):
    cols, reps = lax.axis_size("col"), lax.axis_size("rep")
    if reps != 2 or cols < 2:
        return lax.psum_scatter(parts, ("col", "rep"), scatter_dimension=0)
    shape, kind = parts.shape[1:], parts.dtype
    pieces, _ = chunks_of(shape[0])
    dma = pltpu.SemaphoreType.DMA
    return pl.pallas_call(
        scatter_kernel,
        out_shape=jax.ShapeDtypeStruct(shape, kind),
        in_specs=[pl.BlockSpec(memory_space=pltpu.VMEM)],
        out_specs=pl.BlockSpec(memory_space=pltpu.VMEM),
        scratch_shapes=[
            pltpu.VMEM((cols,) + shape, kind),
            pltpu.VMEM((cols - 1,) + shape, kind),
            pltpu.VMEM((cols - 1,) + shape, kind),
            dma((cols, pieces)),
            dma((cols, pieces)),
            dma((cols - 1, pieces)),
            dma((cols - 1, pieces)),
        ],
        compiler_params=pltpu.CompilerParams(
            collective_id=collective_id, has_side_effects=True, vmem_limit_bytes=VMEM_LIMIT
        ),
        name="scatter",
    )(parts)


def swap_kernel(p_ref, out_ref, send, recv, local):
    cols, reps, c, r = position()
    me = c * reps + r
    pairs = [(d, e) for d in range(cols - 1, -1, -1) for e in range(reps) if (d, e) != (0, 0)]
    places = [(lax.rem(c + d, cols), lax.rem(r + e, reps)) for d, e in pairs]
    greet([{"col": x, "rep": y} for x, y in places])
    copies = []
    for i, (x, y) in enumerate(places):
        copy = remote(
            p_ref.at[x * reps + y], out_ref.at[me], send.at[i], recv.at[i], {"col": x, "rep": y}
        )
        copy.start()
        copies.append(copy)
    keep = pltpu.make_async_copy(p_ref.at[me], out_ref.at[me], local)
    keep.start()
    keep.wait()
    for copy in copies:
        copy.wait()


def swap(parts, collective_id):
    count = parts.shape[0]
    if count < 2:
        return parts
    dma = pltpu.SemaphoreType.DMA
    return pl.pallas_call(
        swap_kernel,
        out_shape=jax.ShapeDtypeStruct(parts.shape, parts.dtype),
        in_specs=[pl.BlockSpec(memory_space=pltpu.VMEM)],
        out_specs=pl.BlockSpec(memory_space=pltpu.VMEM),
        scratch_shapes=[dma((count - 1,)), dma((count - 1,)), dma],
        compiler_params=pltpu.CompilerParams(
            collective_id=collective_id, has_side_effects=True, vmem_limit_bytes=VMEM_LIMIT
        ),
        name="swap",
    )(parts)


def attention_layer(slots, layer, w_qkv, whole_out, attn_gain, first_id):
    group, rows, width = slots.shape
    attended = attend(slots, attn_gain[layer], w_qkv[layer])
    share = rows // group
    mine = swap(attended.reshape(group, share, attended.shape[1]), first_id)
    mine = mine.transpose(1, 0, 2).reshape(share, -1)
    own = lax.dynamic_slice_in_dim(slots, lax.axis_index(("col", "rep")) * share, share, 1)
    own = own.transpose(1, 0, 2).reshape(share, -1)
    return gather(own + matmul(mine, whole_out[layer]), first_id + 1).reshape(rows, -1)


def mlp_kernel(x_ref, gain_ref, up_ref, down_ref, share, out_ref):
    x = x_ref[...]
    hidden = dot3(split(layer_norm(x, gain_ref[...])), split(up_ref[...]))
    hidden = 0.5 * hidden * (1.0 + lax.erf(hidden * (0.5**0.5)))
    total = dot3(split(hidden), split(down_ref[...])) + x * share
    width = out_ref.shape[-1]
    for j in range(out_ref.shape[0]):
        out_ref[j] = total[:, j * width : (j + 1) * width]


def mlp_partial(stream, layer, w_up, w_down, mlp_gain, slots):
    rows, width = stream.shape
    tile = min(256, rows)
    hidden = w_up.shape[-1]
    group = lax.axis_size("col") * lax.axis_size("rep")

    def kernel(x_ref, gain_ref, up_ref, down_ref, out_ref):
        mlp_kernel(x_ref, gain_ref, up_ref, down_ref, 1.0 / group, out_ref)

    return pl.pallas_call(
        kernel,
        grid=(rows // tile,),
        in_specs=[
            pl.BlockSpec((tile, width), lambda i: (i, 0)),
            pl.BlockSpec((1, width), lambda i: (0, 0)),
            pl.BlockSpec((width, hidden), lambda i: (0, 0)),
            pl.BlockSpec((hidden, width), lambda i: (0, 0)),
        ],
        out_specs=pl.BlockSpec((slots, tile, width // slots), lambda i: (0, i, 0)),
        out_shape=jax.ShapeDtypeStruct((slots, rows, width // slots), jnp.float32),
        compiler_params=pltpu.CompilerParams(vmem_limit_bytes=48 * 1024 * 1024),
        name="mlp",
    )(stream, mlp_gain[layer][None, :], w_up[layer], w_down[layer])


def send_blocks(block_list, dest_device, dest_slot):
    block_count, rows_per_block, feature_width = block_list.shape
    peers = lax.axis_size("tok")
    capacity = max(2, (block_count + peers - 4) // (peers - 1))
    order_index = jnp.arange(block_count, dtype=jnp.int32)
    earlier = (dest_device[:, None] == dest_device[None, :]) & (
        order_index[None, :] < order_index[:, None]
    )
    prior_count = jnp.sum(earlier.astype(jnp.int32), axis=1)
    slot_key = dest_device * capacity + prior_count
    select_entries = (
        jnp.arange(peers * capacity, dtype=jnp.int32)[:, None] == slot_key[None, :]
    ).astype(jnp.float32)
    outgoing = jnp.einsum(
        "jb,brf->jrf", select_entries, block_list, precision=MATMUL_PRECISION
    ).reshape(peers, capacity, rows_per_block, feature_width)
    slot_codes = matmul(select_entries, (dest_slot + 1).astype(jnp.float32)).reshape(
        peers, capacity
    )
    incoming, arrived = (
        lax.all_to_all(outgoing, "tok", split_axis=0, concat_axis=0, tiled=True),
        lax.all_to_all(slot_codes, "tok", split_axis=0, concat_axis=0, tiled=True),
    )
    wanted = (order_index + 1).astype(jnp.float32)
    placing = (wanted[:, None] == arrived.reshape(-1)[None, :]).astype(jnp.float32)
    flat_incoming = incoming.reshape(peers * capacity, rows_per_block, feature_width)
    return jnp.einsum("sj,jrf->srf", placing, flat_incoming, precision=MATMUL_PRECISION)


def raster_cells(extended, depth_weight, point_weight, gain_row):
    row_count = extended.shape[0] - 2
    col_count = extended.shape[1] - 2
    channels = extended.shape[2]
    normed = (
        extended
        * lax.rsqrt(jnp.mean(extended * extended, axis=-1, keepdims=True) + EPSILON)
        * gain_row
    )
    mixed = jnp.zeros((row_count, col_count, channels), jnp.float32)
    for a in range(3):
        for b in range(3):
            mixed = mixed + normed[a : a + row_count, b : b + col_count] * depth_weight[a, b]
    combined = matmul(mixed.reshape(row_count * col_count, channels), point_weight)
    combined = combined.reshape(row_count, col_count, 2 * channels)
    centre = extended[1:-1, 1:-1]
    return centre + combined[..., :channels] * jax.nn.sigmoid(combined[..., channels:])


HALO = 2


def extended_cells(tok, members, rep_rows, full_width):
    cols, reps = members
    tile = []
    for col in range(cols):
        for rep in range(reps):
            y = rep * rep_rows - HALO + jnp.arange(rep_rows + 2 * HALO, dtype=jnp.int32)[:, None]
            x = col * TC - HALO + jnp.arange(TC + 2 * HALO, dtype=jnp.int32)[None, :]
            good = (y >= 0) & (y < TR) & (x >= 0) & (x < full_width)
            tile.append(jnp.where(good, (tok * TR + y) * full_width + x, -2).reshape(-1))
    return jnp.concatenate(tile)


def pool(partial, pillar, cells):
    onehot = (cells[:, None] == pillar[None, :]).astype(jnp.float32)
    return matmul(onehot, partial)


def exchange_rows(tile, ntok, reps):
    count = ntok * reps
    rep = lax.axis_index("rep")
    forward = [(i, i + 1) for i in range(count - 1)]
    backward = [(i + 1, i) for i in range(count - 1)]
    above = lax.ppermute(tile[-2 * HALO : -HALO], ("tok", "rep"), forward)
    below = lax.ppermute(tile[HALO : 2 * HALO], ("tok", "rep"), backward)
    above = jnp.where(rep == 0, above, tile[:HALO])
    below = jnp.where(rep == reps - 1, below, tile[-HALO:])
    return jnp.concatenate([above, tile[HALO:-HALO], below], axis=0)


def on_device(
    tokens,
    w_qkv,
    w_out,
    w_up,
    w_down,
    attn_gain,
    mlp_gain,
    dest_device,
    dest_slot,
    pillar,
    depth_weight,
    point_weight,
    raster_gain,
):
    members = (lax.axis_size("col"), lax.axis_size("rep"))
    group = members[0] * members[1]
    ntok = lax.axis_size("tok")
    whole_out = lax.all_gather(w_out, ("col", "rep"), axis=1, tiled=True)
    slots = gather(tokens, 1)
    stream = attention_layer(slots, 0, w_qkv, whole_out, attn_gain, 2)
    share = scatter(mlp_partial(stream, 0, w_up, w_down, mlp_gain, group), 4)
    width = share.shape[1]
    block_count = dest_device.shape[0]
    block_list = share.reshape(block_count, -1, width)
    moved = send_blocks(block_list, dest_device, dest_slot).reshape(-1, width)
    slots = gather(moved, 5)
    stream = attention_layer(slots, 1, w_qkv, whole_out, attn_gain, 6)
    partial = mlp_partial(stream, 1, w_up, w_down, mlp_gain, 1)[0]

    rep_rows = TR // members[1]
    full_width = TC * members[0]
    cells = extended_cells(lax.axis_index("tok"), members, rep_rows, full_width)
    pooled = pool(partial, pillar, cells)
    tile = scatter(pooled.reshape(group, -1, pooled.shape[1]), 8)
    tile = tile.reshape(rep_rows + 2 * HALO, TC + 2 * HALO, -1)
    tile = exchange_rows(tile, ntok, members[1])
    first = raster_cells(tile, depth_weight[0], point_weight[0], raster_gain[0])
    y = lax.axis_index(("tok", "rep")) * rep_rows - 1 + jnp.arange(rep_rows + 2)[:, None, None]
    x = lax.axis_index("col") * TC - 1 + jnp.arange(TC + 2)[None, :, None]
    inside = (y >= 0) & (y < TR * ntok) & (x >= 0) & (x < full_width)
    first = jnp.where(inside, first, 0.0)
    return raster_cells(first, depth_weight[1], point_weight[1], raster_gain[1])


def solution(mesh):
    placed = (
        P(("scene", "tok"), ("col", "rep")),
        P(None, None, None, ("col", "rep")),
        P(None, ("col", "rep"), None),
        P(None, None, ("col", "rep")),
        P(None, ("col", "rep"), None),
        P(),
        P(),
        P(("scene", "tok")),
        P(("scene", "tok")),
        P(("scene", "tok")),
        P(),
        P(),
        P(),
    )
    return jax.shard_map(
        on_device,
        mesh=mesh,
        in_specs=placed,
        out_specs=P(("scene", "tok", "rep"), "col", None),
        check_vma=False,
    )
```

```python
import functools
import math

import jax
import jax.numpy as jnp
from jax import lax
from jax.experimental import pallas as pl
from jax.experimental.pallas import tpu as pltpu
from jax.sharding import PartitionSpec as P

PATCH = 1024
TR = 16
TC = 16
HD = 16


MATMUL_PRECISION = lax.Precision.HIGH
EPSILON = 1e-05


def layer_norm(values, gain_row):
    average = jnp.mean(values, axis=-1, keepdims=True)
    centered = values - average
    variance = jnp.mean(centered * centered, axis=-1, keepdims=True)
    return centered * lax.rsqrt(variance + EPSILON) * gain_row


def split(values):
    high = values.astype(jnp.bfloat16)
    return high, (values - high.astype(jnp.float32)).astype(jnp.bfloat16)


def bdot(left, right, dims=(((1,), (0,)), ((), ()))):
    return lax.dot_general(left, right, dims, preferred_element_type=jnp.float32)


def dot3(left, right):
    lh, ll = left
    rh, rl = right
    return bdot(lh, rh) + bdot(lh, rl) + bdot(ll, rh)


def attention_kernel(share, source_ref, x_ref, gain_ref, w_ref, o_ref, out_ref, q_s, k_s, v_s, att_s):
    cols = w_ref.shape[-1]
    heads = cols // HD
    rows = out_ref.shape[0]
    chunk = att_s.shape[0]
    slots, each, block = x_ref.shape[1:4]
    first_block = pl.program_id(0) * (rows // block)

    def stream_rows(i):
        parts = []
        for n in range(chunk // block):
            at = source_ref[first_block + i * (chunk // block) + n]
            places = [x_ref[at // each, j, at % each] for j in range(slots)]
            parts.append(jnp.concatenate(places, axis=-1))
        return jnp.concatenate(parts, axis=0)

    lanes = q_s.shape[-1]

    r = lax.broadcasted_iota(jnp.int32, (cols, lanes), 0)
    c = lax.broadcasted_iota(jnp.int32, (cols, lanes), 1)
    lane = lax.broadcasted_iota(jnp.int32, (1, cols), 1)
    w = [split(w_ref[j]) for j in range(3)]
    for i in range(rows // chunk):
        at = pl.ds(i * chunk, chunk)
        normed = split(layer_norm(stream_rows(i), gain_ref[...]))
        qh, ql = split(dot3(normed, w[0]) * (HD ** (-0.5) * math.log2(math.e)))
        kh, kl = split(dot3(normed, w[1]))
        vh, vl = split(dot3(normed, w[2]))
        for h in range(heads):
            part = c // HD
            inside = (r // HD == h) & (r % HD == c % HD)
            first = (inside & ((part == 0) | (part == 1))).astype(jnp.bfloat16)
            third = (inside & (part == 2)).astype(jnp.bfloat16)
            outer = (inside & ((part == 0) | (part == 2))).astype(jnp.bfloat16)
            middle = (inside & (part == 1)).astype(jnp.bfloat16)
            q_s[h, at, :] = (bdot(qh, first) + bdot(ql, third)).astype(jnp.bfloat16)
            k_s[h, at, :] = (bdot(kh, outer) + bdot(kl, middle)).astype(jnp.bfloat16)
            own = lane // HD == h
            v_s[h, at, :cols] = jnp.where(own, vh.astype(jnp.float32), 0.0).astype(jnp.bfloat16)
            v_s[h, at, cols:] = jnp.where(own, vl.astype(jnp.float32), 1.0).astype(jnp.bfloat16)

    projection = split(o_ref[...])
    for i in range(rows // chunk):
        at = pl.ds(i * chunk, chunk)
        att_s[...] = jnp.zeros_like(att_s)

        def one_head(h, carry):
            scores = bdot(q_s[h, at, :], k_s[h], (((1,), (1,)), ((), ())))
            weights = jnp.exp2(scores - jnp.max(scores, axis=-1, keepdims=True))
            wh, wl = split(weights)
            sums = bdot(wh, v_s[h]) + bdot(wl, v_s[h])
            top, low = sums[:, :cols], sums[:, cols:]
            own = lane // HD == h
            total = jnp.max(jnp.where(own, 0.0, low), axis=-1, keepdims=True)
            att_s[...] += jnp.where(own, (top + low) / total, 0.0)
            return carry

        lax.fori_loop(0, heads, one_head, 0, unroll=2)
        out_ref[at, :] = dot3(split(att_s[...]), projection) + stream_rows(i) * share


def attend(blocks, source, gain_row, weights, w_out, group):
    block, width = blocks.shape[3], blocks.shape[1] * blocks.shape[4]
    rows = source.shape[0] * block
    cols = weights.shape[-1]
    heads = cols // HD
    lanes = max(128, 3 * HD)
    return pl.pallas_call(
        functools.partial(attention_kernel, 1.0 / group),
        grid_spec=pltpu.PrefetchScalarGridSpec(
            num_scalar_prefetch=1,
            grid=(rows // PATCH,),
            in_specs=[
                pl.BlockSpec(blocks.shape, lambda i, source: (0, 0, 0, 0, 0)),
                pl.BlockSpec((1, width), lambda i, source: (0, 0)),
                pl.BlockSpec(weights.shape, lambda i, source: (0, 0, 0)),
                pl.BlockSpec(w_out.shape, lambda i, source: (0, 0)),
            ],
            out_specs=pl.BlockSpec((PATCH, width), lambda i, source: (i, 0)),
            scratch_shapes=[
                pltpu.VMEM((heads, PATCH, lanes), jnp.bfloat16),
                pltpu.VMEM((heads, PATCH, lanes), jnp.bfloat16),
                pltpu.VMEM((heads, PATCH, 2 * cols), jnp.bfloat16),
                pltpu.VMEM((256, cols), jnp.float32),
            ],
        ),
        out_shape=jax.ShapeDtypeStruct((rows, width), jnp.float32),
        compiler_params=pltpu.CompilerParams(vmem_limit_bytes=48 * 1024 * 1024),
        name="attend",
    )(source, blocks, gain_row[None, :], weights, w_out)


def matmul(left, right):
    return jnp.dot(left, right, precision=MATMUL_PRECISION, preferred_element_type=jnp.float32)


VMEM_LIMIT = 56 * 1024 * 1024
MESH = pl.DeviceIdType.MESH


def position():
    cols, reps = lax.axis_size("col"), lax.axis_size("rep")
    return cols, reps, lax.axis_index("col"), lax.axis_index("rep")


def greet(devices):
    barrier = pltpu.get_barrier_semaphore()
    for device in devices:
        pl.semaphore_signal(barrier, inc=1, device_id=device, device_id_type=MESH)
    pl.semaphore_wait(barrier, len(devices))


def remote(src, dst, send, recv, device):
    return pltpu.make_async_remote_copy(
        src_ref=src, dst_ref=dst, send_sem=send, recv_sem=recv, device_id=device, device_id_type=MESH
    )


def chunks_of(rows):
    pieces = 4 if rows % 64 == 0 else (2 if rows % 16 == 0 else 1)
    return pieces, rows // pieces


def gather_kernel(x_ref, out_ref, xs, xr, fs, fr, ps, pr, local):
    cols, reps, c, r = position()
    rows = x_ref.shape[0]
    pieces, size = chunks_of(rows)
    me = c * reps + r
    mate = {"col": c, "rep": 1 - r}
    others = [{"col": lax.rem(c + d, cols), "rep": r} for d in range(1, cols)]
    greet([mate] + others)
    across, onward = [], []
    for k in range(pieces):
        at = pl.ds(k * size, size)
        for d in range(1, cols):
            copy = remote(
                x_ref.at[at], out_ref.at[me, at], xs.at[d - 1, k], xr.at[d - 1, k], others[d - 1]
            )
            copy.start()
            across.append(copy)
    share = remote(x_ref, out_ref.at[me], ps, pr, mate)
    share.start()
    keep = pltpu.make_async_copy(x_ref, out_ref.at[me], local)
    keep.start()
    for k in range(pieces):
        at = pl.ds(k * size, size)
        for d in range(1, cols):
            across[k * (cols - 1) + d - 1].wait_recv()
            slot = lax.rem(c + cols - d, cols) * reps + r
            copy = remote(
                out_ref.at[slot, at], out_ref.at[slot, at], fs.at[d - 1, k], fr.at[d - 1, k], mate
            )
            copy.start()
            onward.append(copy)
    for copy in across:
        copy.wait_send()
    share.wait()
    keep.wait()
    for copy in onward:
        copy.wait()


def gather(block, collective_id):
    cols, reps = lax.axis_size("col"), lax.axis_size("rep")
    if reps != 2 or cols < 2:
        return lax.all_gather(block, ("col", "rep"), axis=0)
    pieces, _ = chunks_of(block.shape[0])
    dma = pltpu.SemaphoreType.DMA
    return pl.pallas_call(
        gather_kernel,
        out_shape=jax.ShapeDtypeStruct((cols * reps,) + block.shape, block.dtype),
        in_specs=[pl.BlockSpec(memory_space=pltpu.VMEM)],
        out_specs=pl.BlockSpec(memory_space=pltpu.VMEM),
        scratch_shapes=[dma((cols - 1, pieces))] * 4 + [dma, dma, dma],
        compiler_params=pltpu.CompilerParams(
            collective_id=collective_id, has_side_effects=True, vmem_limit_bytes=VMEM_LIMIT
        ),
        name="gather",
    )(block)


def scatter_kernel(p_ref, out_ref, a_ref, s_ref, b_ref, a_s, a_r, b_s, b_r):
    cols, reps, c, r = position()
    rows = p_ref.shape[1]
    pieces, size = chunks_of(rows)
    mate = {"col": c, "rep": 1 - r}
    others = [{"col": lax.rem(c + d, cols), "rep": r} for d in range(1, cols)]
    greet([mate] + others)
    order = [(k, d) for k in range(pieces) for d in range(1, cols)]
    order += [(k, 0) for k in range(pieces)]
    near, far = {}, {}
    for k, d in order:
        at = pl.ds(k * size, size)
        slot = lax.rem(c + d, cols) * reps + 1 - r
        near[k, d] = remote(
            p_ref.at[slot, at], a_ref.at[d, at], a_s.at[d, k], a_r.at[d, k], mate
        )
        near[k, d].start()
    for k, d in order:
        at = pl.ds(k * size, size)
        slot = lax.rem(c + d, cols) * reps + r
        near[k, d].wait_recv()
        total = p_ref[slot, at] + a_ref[d, at]
        if d == 0:
            out_ref[at] = total
        else:
            s_ref[d - 1, at] = total
            far[k, d] = remote(
                s_ref.at[d - 1, at],
                b_ref.at[d - 1, at],
                b_s.at[d - 1, k],
                b_r.at[d - 1, k],
                others[d - 1],
            )
            far[k, d].start()
    for (k, d), copy in far.items():
        at = pl.ds(k * size, size)
        copy.wait_recv()
        out_ref[at] += b_ref[d - 1, at]
    for copy in list(near.values()) + list(far.values()):
        copy.wait_send()


def scatter(parts, collective_id):
    cols, reps = lax.axis_size("col"), lax.axis_size("rep")
    if reps != 2 or cols < 2:
        return lax.psum_scatter(parts, ("col", "rep"), scatter_dimension=0)
    shape, kind = parts.shape[1:], parts.dtype
    pieces, _ = chunks_of(shape[0])
    dma = pltpu.SemaphoreType.DMA
    return pl.pallas_call(
        scatter_kernel,
        out_shape=jax.ShapeDtypeStruct(shape, kind),
        in_specs=[pl.BlockSpec(memory_space=pltpu.VMEM)],
        out_specs=pl.BlockSpec(memory_space=pltpu.VMEM),
        scratch_shapes=[
            pltpu.VMEM((cols,) + shape, kind),
            pltpu.VMEM((cols - 1,) + shape, kind),
            pltpu.VMEM((cols - 1,) + shape, kind),
            dma((cols, pieces)),
            dma((cols, pieces)),
            dma((cols - 1, pieces)),
            dma((cols - 1, pieces)),
        ],
        compiler_params=pltpu.CompilerParams(
            collective_id=collective_id, has_side_effects=True, vmem_limit_bytes=VMEM_LIMIT
        ),
        name="scatter",
    )(parts)


def total_kernel(
    p_ref, out_ref, a_ref, s_ref, b_ref, a_s, a_r, b_s, b_r, xs, xr, fs, fr, ps, pr
):
    cols, reps, c, r = position()
    rows = p_ref.shape[1]
    pieces, size = chunks_of(rows)
    me = c * reps + r
    mate = {"col": c, "rep": 1 - r}
    others = [{"col": lax.rem(c + d, cols), "rep": r} for d in range(1, cols)]
    greet([mate] + others)
    order = [(k, d) for k in range(pieces) for d in range(1, cols)]
    order += [(k, 0) for k in range(pieces)]
    near, far, across, share, onward = {}, {}, {}, {}, {}
    for k, d in order:
        at = pl.ds(k * size, size)
        slot = lax.rem(c + d, cols) * reps + 1 - r
        near[k, d] = remote(
            p_ref.at[slot, at], a_ref.at[d, at], a_s.at[d, k], a_r.at[d, k], mate
        )
        near[k, d].start()
    for k, d in order:
        if d == 0:
            continue
        at = pl.ds(k * size, size)
        slot = lax.rem(c + d, cols) * reps + r
        near[k, d].wait_recv()
        s_ref[d - 1, at] = p_ref[slot, at] + a_ref[d, at]
        far[k, d] = remote(
            s_ref.at[d - 1, at], b_ref.at[d - 1, at], b_s.at[d - 1, k], b_r.at[d - 1, k], others[d - 1]
        )
        far[k, d].start()
    for k in range(pieces):
        at = pl.ds(k * size, size)
        near[k, 0].wait_recv()
        total = p_ref[me, at] + a_ref[0, at]
        for d in range(1, cols):
            far[k, d].wait_recv()
            total = total + b_ref[d - 1, at]
        out_ref[me, at] = total
        for d in range(1, cols):
            across[k, d] = remote(
                out_ref.at[me, at], out_ref.at[me, at], xs.at[d - 1, k], xr.at[d - 1, k], others[d - 1]
            )
            across[k, d].start()
        share[k] = remote(out_ref.at[me, at], out_ref.at[me, at], ps.at[k], pr.at[k], mate)
        share[k].start()
    for (k, d), copy in across.items():
        at = pl.ds(k * size, size)
        copy.wait_recv()
        slot = lax.rem(c + cols - d, cols) * reps + r
        onward[k, d] = remote(
            out_ref.at[slot, at], out_ref.at[slot, at], fs.at[d - 1, k], fr.at[d - 1, k], mate
        )
        onward[k, d].start()
    for copies in (near, far, across):
        for copy in copies.values():
            copy.wait_send()
    for copies in (share, onward):
        for copy in copies.values():
            copy.wait()


def total(parts, collective_id):
    cols, reps = lax.axis_size("col"), lax.axis_size("rep")
    if reps != 2 or cols < 2:
        return lax.psum(parts, ("col", "rep"))
    shape, kind = parts.shape[1:], parts.dtype
    pieces, _ = chunks_of(shape[0])
    dma = pltpu.SemaphoreType.DMA
    return pl.pallas_call(
        total_kernel,
        out_shape=jax.ShapeDtypeStruct(parts.shape, kind),
        in_specs=[pl.BlockSpec(memory_space=pltpu.VMEM)],
        out_specs=pl.BlockSpec(memory_space=pltpu.VMEM),
        scratch_shapes=[
            pltpu.VMEM((cols,) + shape, kind),
            pltpu.VMEM((cols - 1,) + shape, kind),
            pltpu.VMEM((cols - 1,) + shape, kind),
            dma((cols, pieces)),
            dma((cols, pieces)),
        ]
        + [dma((cols - 1, pieces))] * 6
        + [dma((pieces,))] * 2,
        compiler_params=pltpu.CompilerParams(
            collective_id=collective_id, has_side_effects=True, vmem_limit_bytes=VMEM_LIMIT
        ),
        name="total",
    )(parts)


def move_kernel(o_ref, code_ref, out_ref, arrived_ref, zs, zr, cs, cr, xs, xr, fs, fr, ps, pr, local):
    cols, reps, c, r = position()
    ntok, t = lax.axis_size("tok"), lax.axis_index("tok")
    me = c * reps + r
    mate = {"col": c, "rep": 1 - r}
    others = [{"col": lax.rem(c + d, cols), "rep": r} for d in range(1, cols)]
    peers = [{"tok": lax.rem(t + e, ntok)} for e in range(1, ntok)]
    greet([mate] + others + peers)
    along, codes, across, share, onward = [], [], {}, [], []
    for e in range(1, ntok):
        target = lax.rem(t + e, ntok)
        copy = remote(o_ref.at[target], out_ref.at[t, me], zs.at[e - 1], zr.at[e - 1], peers[e - 1])
        copy.start()
        along.append(copy)
        copy = remote(
            code_ref.at[target], arrived_ref.at[t], cs.at[e - 1], cr.at[e - 1], peers[e - 1]
        )
        copy.start()
        codes.append(copy)
    keep = pltpu.make_async_copy(o_ref.at[t], out_ref.at[t, me], local.at[0])
    keep.start()
    keep_code = pltpu.make_async_copy(code_ref.at[t], arrived_ref.at[t], local.at[1])
    keep_code.start()

    def hand_on(e):
        u = lax.rem(t + ntok - e, ntok)
        for d in range(1, cols):
            across[e, d].wait_recv()
            slot = lax.rem(c + cols - d, cols) * reps + r
            copy = remote(
                out_ref.at[u, slot], out_ref.at[u, slot], fs.at[e, d - 1], fr.at[e, d - 1], mate
            )
            copy.start()
            onward.append(copy)

    for e in range(ntok):
        u = lax.rem(t + ntok - e, ntok)
        if e:
            along[e - 1].wait_recv()
        origin = out_ref.at[u, me] if e else o_ref.at[t]
        for d in range(1, cols):
            across[e, d] = remote(
                origin, out_ref.at[u, me], xs.at[e, d - 1], xr.at[e, d - 1], others[d - 1]
            )
            across[e, d].start()
        copy = remote(origin, out_ref.at[u, me], ps.at[e], pr.at[e], mate)
        copy.start()
        share.append(copy)
        if e:
            hand_on(e - 1)
    hand_on(ntok - 1)
    keep.wait()
    keep_code.wait()
    for copy in along + list(across.values()):
        copy.wait_send()
    for copy in codes + share + onward:
        copy.wait()


def move(outgoing, codes, collective_id):
    cols, reps, ntok = lax.axis_size("col"), lax.axis_size("rep"), lax.axis_size("tok")
    if reps != 2 or cols < 2 or ntok < 2:
        incoming = lax.all_to_all(outgoing, "tok", split_axis=0, concat_axis=0, tiled=True)
        arrived = lax.all_to_all(codes, "tok", split_axis=0, concat_axis=0, tiled=True)
        return lax.all_gather(incoming, ("col", "rep"), axis=1), arrived
    dma = pltpu.SemaphoreType.DMA
    shape = (ntok, cols * reps) + outgoing.shape[1:]
    return pl.pallas_call(
        move_kernel,
        out_shape=(
            jax.ShapeDtypeStruct(shape, outgoing.dtype),
            jax.ShapeDtypeStruct(codes.shape, codes.dtype),
        ),
        in_specs=[pl.BlockSpec(memory_space=pltpu.VMEM)] * 2,
        out_specs=[pl.BlockSpec(memory_space=pltpu.VMEM)] * 2,
        scratch_shapes=[dma((ntok - 1,))] * 4
        + [dma((ntok, cols - 1))] * 4
        + [dma((ntok,))] * 2
        + [dma((2,))],
        compiler_params=pltpu.CompilerParams(
            collective_id=collective_id, has_side_effects=True, vmem_limit_bytes=VMEM_LIMIT
        ),
        name="move",
    )(outgoing, codes)


def pick_kernel(index_ref, x_ref, out_ref):
    for j in range(out_ref.shape[0]):
        out_ref[j] = x_ref[index_ref[j]]


def pick(blocks, index):
    return pl.pallas_call(
        pick_kernel,
        out_shape=jax.ShapeDtypeStruct(index.shape + blocks.shape[1:], blocks.dtype),
        in_specs=[pl.BlockSpec(memory_space=pltpu.SMEM), pl.BlockSpec(memory_space=pltpu.VMEM)],
        out_specs=pl.BlockSpec(memory_space=pltpu.VMEM),
        name="pick",
    )(index, blocks)


def attention_layer(blocks, source, layer, w_qkv, w_out, attn_gain, collective_id):
    group = blocks.shape[1]
    terms = attend(blocks, source, attn_gain[layer], w_qkv[layer], w_out[layer], group)
    rows, width = terms.shape
    return total(terms.reshape(group, rows // group, width), collective_id).reshape(rows, width)


def mlp_kernel(x_ref, gain_ref, up_ref, down_ref, share, out_ref):
    x = x_ref[...]
    hidden = dot3(split(layer_norm(x, gain_ref[...])), split(up_ref[...]))
    hidden = 0.5 * hidden * (1.0 + lax.erf(hidden * (0.5**0.5)))
    total = dot3(split(hidden), split(down_ref[...])) + x * share
    width = out_ref.shape[-1]
    for j in range(out_ref.shape[0]):
        out_ref[j] = total[:, j * width : (j + 1) * width]


def mlp_partial(stream, layer, w_up, w_down, mlp_gain, slots):
    rows, width = stream.shape
    tile = min(256, rows)
    hidden = w_up.shape[-1]
    group = lax.axis_size("col") * lax.axis_size("rep")

    def kernel(x_ref, gain_ref, up_ref, down_ref, out_ref):
        mlp_kernel(x_ref, gain_ref, up_ref, down_ref, 1.0 / group, out_ref)

    return pl.pallas_call(
        kernel,
        grid=(rows // tile,),
        in_specs=[
            pl.BlockSpec((tile, width), lambda i: (i, 0)),
            pl.BlockSpec((1, width), lambda i: (0, 0)),
            pl.BlockSpec((width, hidden), lambda i: (0, 0)),
            pl.BlockSpec((hidden, width), lambda i: (0, 0)),
        ],
        out_specs=pl.BlockSpec((slots, tile, width // slots), lambda i: (0, i, 0)),
        out_shape=jax.ShapeDtypeStruct((slots, rows, width // slots), jnp.float32),
        compiler_params=pltpu.CompilerParams(vmem_limit_bytes=48 * 1024 * 1024),
        name="mlp",
    )(stream, mlp_gain[layer][None, :], w_up[layer], w_down[layer])


def routes(dest_device, dest_slot):
    count = dest_device.shape[0]
    peers = lax.axis_size("tok")
    capacity = max(2, (count + peers - 4) // (peers - 1))
    order = jnp.arange(count, dtype=jnp.int32)
    earlier = (dest_device[:, None] == dest_device[None, :]) & (order[None, :] < order[:, None])
    place = dest_device * capacity + jnp.sum(earlier.astype(jnp.int32), axis=1)
    chosen = jnp.arange(peers * capacity, dtype=jnp.int32)[:, None] == place[None, :]
    index = jnp.sum(jnp.where(chosen, order[None, :], 0), axis=1)
    code = jnp.sum(jnp.where(chosen, dest_slot[None, :] + 1, 0), axis=1)
    code = jnp.pad(code.reshape(peers, capacity), ((0, 0), (0, 128 - capacity)))
    code = jnp.broadcast_to(code[:, None, :], (peers, 8, 128)).astype(jnp.float32)
    return index, code, capacity


def raster_cells(extended, depth_weight, point_weight, gain_row):
    row_count = extended.shape[0] - 2
    col_count = extended.shape[1] - 2
    channels = extended.shape[2]
    normed = (
        extended
        * lax.rsqrt(jnp.mean(extended * extended, axis=-1, keepdims=True) + EPSILON)
        * gain_row
    )
    mixed = jnp.zeros((row_count, col_count, channels), jnp.float32)
    for a in range(3):
        for b in range(3):
            mixed = mixed + normed[a : a + row_count, b : b + col_count] * depth_weight[a, b]
    combined = matmul(mixed.reshape(row_count * col_count, channels), point_weight)
    combined = combined.reshape(row_count, col_count, 2 * channels)
    centre = extended[1:-1, 1:-1]
    return centre + combined[..., :channels] * jax.nn.sigmoid(combined[..., channels:])


HALO = 2


def extended_cells(tok, members, rep_rows, full_width):
    cols, reps = members
    tile = []
    for col in range(cols):
        for rep in range(reps):
            y = rep * rep_rows - HALO + jnp.arange(rep_rows + 2 * HALO, dtype=jnp.int32)[:, None]
            x = col * TC - HALO + jnp.arange(TC + 2 * HALO, dtype=jnp.int32)[None, :]
            good = (y >= 0) & (y < TR) & (x >= 0) & (x < full_width)
            tile.append(jnp.where(good, (tok * TR + y) * full_width + x, -2).reshape(-1))
    return jnp.concatenate(tile)


def pool(partial, pillar, cells):
    onehot = (cells[:, None] == pillar[None, :]).astype(jnp.float32)
    return matmul(onehot, partial)


def exchange_rows(tile, ntok, reps):
    count = ntok * reps
    rep = lax.axis_index("rep")
    forward = [(i, i + 1) for i in range(count - 1)]
    backward = [(i + 1, i) for i in range(count - 1)]
    above = lax.ppermute(tile[-2 * HALO : -HALO], ("tok", "rep"), forward)
    below = lax.ppermute(tile[HALO : 2 * HALO], ("tok", "rep"), backward)
    above = jnp.where(rep == 0, above, tile[:HALO])
    below = jnp.where(rep == reps - 1, below, tile[-HALO:])
    return jnp.concatenate([above, tile[HALO:-HALO], below], axis=0)


def on_device(
    tokens,
    w_qkv,
    w_out,
    w_up,
    w_down,
    attn_gain,
    mlp_gain,
    dest_device,
    dest_slot,
    pillar,
    depth_weight,
    point_weight,
    raster_gain,
):
    members = (lax.axis_size("col"), lax.axis_size("rep"))
    group = members[0] * members[1]
    ntok = lax.axis_size("tok")
    block_count = dest_device.shape[0]
    order = jnp.arange(block_count, dtype=jnp.int32)
    index, codes, capacity = routes(dest_device, dest_slot)
    width = tokens.shape[1]
    blocks = gather(tokens, 1).reshape(1, group, block_count, -1, width)
    stream = attention_layer(blocks, order, 0, w_qkv, w_out, attn_gain, 2)
    share = scatter(mlp_partial(stream, 0, w_up, w_down, mlp_gain, group), 3)
    outgoing = pick(share.reshape(block_count, -1, width), index)
    outgoing = outgoing.reshape(ntok, -1, width)
    moved, arrived = move(outgoing, codes, 4)
    blocks = moved.reshape(ntok, group, capacity, -1, width)
    held = arrived[:, 0, :capacity].reshape(-1).astype(jnp.int32)
    found = held[None, :] == order[:, None] + 1
    source = jnp.sum(jnp.where(found, jnp.arange(held.shape[0], dtype=jnp.int32)[None, :], 0), axis=1)
    stream = attention_layer(blocks, source, 1, w_qkv, w_out, attn_gain, 5)
    partial = mlp_partial(stream, 1, w_up, w_down, mlp_gain, 1)[0]

    rep_rows = TR // members[1]
    full_width = TC * members[0]
    cells = extended_cells(lax.axis_index("tok"), members, rep_rows, full_width)
    pooled = pool(partial, pillar, cells)
    tile = scatter(pooled.reshape(group, -1, pooled.shape[1]), 6)
    tile = tile.reshape(rep_rows + 2 * HALO, TC + 2 * HALO, -1)
    tile = exchange_rows(tile, ntok, members[1])
    first = raster_cells(tile, depth_weight[0], point_weight[0], raster_gain[0])
    y = lax.axis_index(("tok", "rep")) * rep_rows - 1 + jnp.arange(rep_rows + 2)[:, None, None]
    x = lax.axis_index("col") * TC - 1 + jnp.arange(TC + 2)[None, :, None]
    inside = (y >= 0) & (y < TR * ntok) & (x >= 0) & (x < full_width)
    first = jnp.where(inside, first, 0.0)
    return raster_cells(first, depth_weight[1], point_weight[1], raster_gain[1])


def solution(mesh):
    placed = (
        P(("scene", "tok"), ("col", "rep")),
        P(None, None, None, ("col", "rep")),
        P(None, ("col", "rep"), None),
        P(None, None, ("col", "rep")),
        P(None, ("col", "rep"), None),
        P(),
        P(),
        P(("scene", "tok")),
        P(("scene", "tok")),
        P(("scene", "tok")),
        P(),
        P(),
        P(),
    )
    return jax.shard_map(
        on_device,
        mesh=mesh,
        in_specs=placed,
        out_specs=P(("scene", "tok", "rep"), "col", None),
        check_vma=False,
    )
```

```python
import functools
import math

import jax
import jax.numpy as jnp
from jax import lax
from jax.experimental import pallas as pl
from jax.experimental.pallas import tpu as pltpu
from jax.sharding import PartitionSpec as P

PATCH = 1024
TR = 16
TC = 16
HD = 16


MATMUL_PRECISION = lax.Precision.HIGH
EPSILON = 1e-05


def layer_norm(values, gain_row):
    average = jnp.mean(values, axis=-1, keepdims=True)
    centered = values - average
    variance = jnp.mean(centered * centered, axis=-1, keepdims=True)
    return centered * lax.rsqrt(variance + EPSILON) * gain_row


def split(values):
    high = values.astype(jnp.bfloat16)
    return high, (values - high.astype(jnp.float32)).astype(jnp.bfloat16)


def bdot(left, right, dims=(((1,), (0,)), ((), ()))):
    return lax.dot_general(left, right, dims, preferred_element_type=jnp.float32)


def dot3(left, right):
    lh, ll = left
    rh, rl = right
    return bdot(lh, rh) + bdot(lh, rl) + bdot(ll, rh)


def attention_kernel(share, source_ref, x_ref, gain_ref, w_ref, o_ref, out_ref, q_s, k_s, v_s, att_s):
    cols = w_ref.shape[-1]
    heads = cols // HD
    rows = out_ref.shape[0]
    chunk = att_s.shape[0]
    slots, each, block = x_ref.shape[1:4]
    first_block = pl.program_id(0) * (rows // block)

    def stream_rows(i):
        parts = []
        for n in range(chunk // block):
            at = source_ref[first_block + i * (chunk // block) + n]
            places = [x_ref[at // each, j, at % each] for j in range(slots)]
            parts.append(jnp.concatenate(places, axis=-1))
        return jnp.concatenate(parts, axis=0)

    lanes = q_s.shape[-1]

    r = lax.broadcasted_iota(jnp.int32, (cols, lanes), 0)
    c = lax.broadcasted_iota(jnp.int32, (cols, lanes), 1)
    lane = lax.broadcasted_iota(jnp.int32, (1, cols), 1)
    w = [split(w_ref[j]) for j in range(3)]
    for i in range(rows // chunk):
        at = pl.ds(i * chunk, chunk)
        normed = split(layer_norm(stream_rows(i), gain_ref[...]))
        qh, ql = split(dot3(normed, w[0]) * (HD ** (-0.5) * math.log2(math.e)))
        kh, kl = split(dot3(normed, w[1]))
        vh, vl = split(dot3(normed, w[2]))
        for h in range(heads):
            part = c // HD
            inside = (r // HD == h) & (r % HD == c % HD)
            first = (inside & ((part == 0) | (part == 1))).astype(jnp.bfloat16)
            third = (inside & (part == 2)).astype(jnp.bfloat16)
            outer = (inside & ((part == 0) | (part == 2))).astype(jnp.bfloat16)
            middle = (inside & (part == 1)).astype(jnp.bfloat16)
            q_s[h, at, :] = (bdot(qh, first) + bdot(ql, third)).astype(jnp.bfloat16)
            k_s[h, at, :] = (bdot(kh, outer) + bdot(kl, middle)).astype(jnp.bfloat16)
            own = lane // HD == h
            v_s[h, at, :cols] = jnp.where(own, vh.astype(jnp.float32), 0.0).astype(jnp.bfloat16)
            v_s[h, at, cols:] = jnp.where(own, vl.astype(jnp.float32), 1.0).astype(jnp.bfloat16)

    projection = split(o_ref[...])

    def query_rows(i, carry):
        at = pl.ds(pl.multiple_of(i * chunk, chunk), chunk)
        att_s[...] = jnp.zeros_like(att_s)

        def one_head(h, carry):
            scores = bdot(q_s[h, at, :], k_s[h], (((1,), (1,)), ((), ())))
            weights = jnp.exp2(scores - jnp.max(scores, axis=-1, keepdims=True))
            wh, wl = split(weights)
            sums = bdot(wh, v_s[h]) + bdot(wl, v_s[h])
            top, low = sums[:, :cols], sums[:, cols:]
            own = lane // HD == h
            total = jnp.max(jnp.where(own, 0.0, low), axis=-1, keepdims=True)
            att_s[...] += jnp.where(own, (top + low) / total, 0.0)
            return carry

        lax.fori_loop(0, heads, one_head, 0, unroll=4)
        out_ref[at, :] = dot3(split(att_s[...]), projection) + stream_rows(i) * share
        return carry

    lax.fori_loop(0, rows // chunk, query_rows, 0)


def attend(blocks, source, gain_row, weights, w_out, group):
    block, width = blocks.shape[3], blocks.shape[1] * blocks.shape[4]
    rows = source.shape[0] * block
    cols = weights.shape[-1]
    heads = cols // HD
    lanes = max(128, 3 * HD)
    return pl.pallas_call(
        functools.partial(attention_kernel, 1.0 / group),
        grid_spec=pltpu.PrefetchScalarGridSpec(
            num_scalar_prefetch=1,
            grid=(rows // PATCH,),
            in_specs=[
                pl.BlockSpec(blocks.shape, lambda i, source: (0, 0, 0, 0, 0)),
                pl.BlockSpec((1, width), lambda i, source: (0, 0)),
                pl.BlockSpec(weights.shape, lambda i, source: (0, 0, 0)),
                pl.BlockSpec(w_out.shape, lambda i, source: (0, 0)),
            ],
            out_specs=pl.BlockSpec((PATCH, width), lambda i, source: (i, 0)),
            scratch_shapes=[
                pltpu.VMEM((heads, PATCH, lanes), jnp.bfloat16),
                pltpu.VMEM((heads, PATCH, lanes), jnp.bfloat16),
                pltpu.VMEM((heads, PATCH, 2 * cols), jnp.bfloat16),
                pltpu.VMEM((256, cols), jnp.float32),
            ],
        ),
        out_shape=jax.ShapeDtypeStruct((rows, width), jnp.float32),
        compiler_params=pltpu.CompilerParams(vmem_limit_bytes=48 * 1024 * 1024),
        name="attend",
    )(source, blocks, gain_row[None, :], weights, w_out)


def matmul(left, right):
    return jnp.dot(left, right, precision=MATMUL_PRECISION, preferred_element_type=jnp.float32)


VMEM_LIMIT = 56 * 1024 * 1024
MESH = pl.DeviceIdType.MESH


def position():
    cols, reps = lax.axis_size("col"), lax.axis_size("rep")
    return cols, reps, lax.axis_index("col"), lax.axis_index("rep")


def greet(devices):
    barrier = pltpu.get_barrier_semaphore()
    for device in devices:
        pl.semaphore_signal(barrier, inc=1, device_id=device, device_id_type=MESH)
    pl.semaphore_wait(barrier, len(devices))


def remote(src, dst, send, recv, device):
    return pltpu.make_async_remote_copy(
        src_ref=src, dst_ref=dst, send_sem=send, recv_sem=recv, device_id=device, device_id_type=MESH
    )


def chunks_of(rows):
    for pieces in (8, 5, 4, 2):
        if rows % (8 * pieces) == 0:
            return pieces, rows // pieces
    return 1, rows


def gather_kernel(x_ref, out_ref, xs, xr, fs, fr, ps, pr, local):
    cols, reps, c, r = position()
    rows = x_ref.shape[0]
    pieces, size = chunks_of(rows)
    me = c * reps + r
    mate = {"col": c, "rep": 1 - r}
    others = [{"col": lax.rem(c + d, cols), "rep": r} for d in range(1, cols)]
    greet([mate] + others)
    across, onward = [], []
    for k in range(pieces):
        at = pl.ds(k * size, size)
        for d in range(1, cols):
            copy = remote(
                x_ref.at[at], out_ref.at[me, at], xs.at[d - 1, k], xr.at[d - 1, k], others[d - 1]
            )
            copy.start()
            across.append(copy)
    share = remote(x_ref, out_ref.at[me], ps, pr, mate)
    share.start()
    keep = pltpu.make_async_copy(x_ref, out_ref.at[me], local)
    keep.start()
    for k in range(pieces):
        at = pl.ds(k * size, size)
        for d in range(1, cols):
            across[k * (cols - 1) + d - 1].wait_recv()
            slot = lax.rem(c + cols - d, cols) * reps + r
            copy = remote(
                out_ref.at[slot, at], out_ref.at[slot, at], fs.at[d - 1, k], fr.at[d - 1, k], mate
            )
            copy.start()
            onward.append(copy)
    for copy in across:
        copy.wait_send()
    share.wait()
    keep.wait()
    for copy in onward:
        copy.wait()


def gather(block, collective_id):
    cols, reps = lax.axis_size("col"), lax.axis_size("rep")
    if reps != 2 or cols < 2:
        return lax.all_gather(block, ("col", "rep"), axis=0)
    pieces, _ = chunks_of(block.shape[0])
    dma = pltpu.SemaphoreType.DMA
    return pl.pallas_call(
        gather_kernel,
        out_shape=jax.ShapeDtypeStruct((cols * reps,) + block.shape, block.dtype),
        in_specs=[pl.BlockSpec(memory_space=pltpu.VMEM)],
        out_specs=pl.BlockSpec(memory_space=pltpu.VMEM),
        scratch_shapes=[dma((cols - 1, pieces))] * 4 + [dma, dma, dma],
        compiler_params=pltpu.CompilerParams(
            collective_id=collective_id, has_side_effects=True, vmem_limit_bytes=VMEM_LIMIT
        ),
        name="gather",
    )(block)


def scatter_kernel(edge, p_ref, out_ref, a_ref, s_ref, b_ref, a_s, a_r, b_s, b_r, *halo):
    cols, reps, c, r = position()
    rows = p_ref.shape[1]
    pieces, size = chunks_of(rows)
    mate = {"col": c, "rep": 1 - r}
    others = [{"col": lax.rem(c + d, cols), "rep": r} for d in range(1, cols)]
    greeted = [mate] + others
    if edge:
        ntok, t = lax.axis_size("tok"), lax.axis_index("tok")
        partner = {"tok": lax.rem(t + jnp.where(r == 0, ntok - 1, 1), ntok), "rep": 1 - r}
        greeted = greeted + [partner]
    greet(greeted)
    order = [(k, d) for k in range(pieces) for d in range(1, cols)]
    order += [(k, 0) for k in range(pieces)]
    near, far = {}, {}
    for k, d in order:
        at = pl.ds(k * size, size)
        slot = lax.rem(c + d, cols) * reps + 1 - r
        near[k, d] = remote(
            p_ref.at[slot, at], a_ref.at[d, at], a_s.at[d, k], a_r.at[d, k], mate
        )
        near[k, d].start()
    for k, d in order:
        at = pl.ds(k * size, size)
        slot = lax.rem(c + d, cols) * reps + r
        near[k, d].wait_recv()
        total = p_ref[slot, at] + a_ref[d, at]
        if d == 0:
            out_ref[at] = total
        else:
            s_ref[d - 1, at] = total
            far[k, d] = remote(
                s_ref.at[d - 1, at],
                b_ref.at[d - 1, at],
                b_s.at[d - 1, k],
                b_r.at[d - 1, k],
                others[d - 1],
            )
            far[k, d].start()
    for (k, d), copy in far.items():
        at = pl.ds(k * size, size)
        copy.wait_recv()
        out_ref[at] += b_ref[d - 1, at]
    if edge:
        h_ref, e_ref, h_s, h_r = halo
        inner = pl.multiple_of(jnp.where(r == 0, edge, rows - 2 * edge), 8)
        outer = pl.multiple_of(jnp.where(r == 0, 0, rows - edge), 8)
        e_ref[...] = out_ref[pl.ds(inner, edge)]
        copy = remote(e_ref, h_ref, h_s, h_r, partner)
        copy.start()
        copy.wait()
        wrapped = jnp.where(r == 0, t == 0, t == ntok - 1)
        out_ref[pl.ds(outer, edge)] = jnp.where(wrapped, 0.0, h_ref[...])
    for copy in list(near.values()) + list(far.values()):
        copy.wait_send()


def scatter(parts, collective_id, edge=0):
    cols, reps = lax.axis_size("col"), lax.axis_size("rep")
    if reps != 2 or cols < 2:
        return lax.psum_scatter(parts, ("col", "rep"), scatter_dimension=0)
    shape, kind = parts.shape[1:], parts.dtype
    pieces, _ = chunks_of(shape[0])
    dma = pltpu.SemaphoreType.DMA
    return pl.pallas_call(
        functools.partial(scatter_kernel, edge),
        out_shape=jax.ShapeDtypeStruct(shape, kind),
        in_specs=[pl.BlockSpec(memory_space=pltpu.VMEM)],
        out_specs=pl.BlockSpec(memory_space=pltpu.VMEM),
        scratch_shapes=[
            pltpu.VMEM((cols,) + shape, kind),
            pltpu.VMEM((cols - 1,) + shape, kind),
            pltpu.VMEM((cols - 1,) + shape, kind),
            dma((cols, pieces)),
            dma((cols, pieces)),
            dma((cols - 1, pieces)),
            dma((cols - 1, pieces)),
        ]
        + ([pltpu.VMEM((edge, shape[1]), kind)] * 2 + [dma, dma] if edge else []),
        compiler_params=pltpu.CompilerParams(
            collective_id=collective_id, has_side_effects=True, vmem_limit_bytes=VMEM_LIMIT
        ),
        name="scatter",
    )(parts)


def total_kernel(
    p_ref, out_ref, a_ref, s_ref, b_ref, a_s, a_r, b_s, b_r, xs, xr, fs, fr, ps, pr
):
    cols, reps, c, r = position()
    rows = p_ref.shape[1]
    pieces, size = chunks_of(rows)
    me = c * reps + r
    mate = {"col": c, "rep": 1 - r}
    others = [{"col": lax.rem(c + d, cols), "rep": r} for d in range(1, cols)]
    greet([mate] + others)
    order = [(k, d) for k in range(pieces) for d in range(1, cols)]
    order += [(k, 0) for k in range(pieces)]
    near, far, across, share, onward = {}, {}, {}, {}, {}
    for k, d in order:
        at = pl.ds(k * size, size)
        slot = lax.rem(c + d, cols) * reps + 1 - r
        near[k, d] = remote(
            p_ref.at[slot, at], a_ref.at[d, at], a_s.at[d, k], a_r.at[d, k], mate
        )
        near[k, d].start()
    for k, d in order:
        if d == 0:
            continue
        at = pl.ds(k * size, size)
        slot = lax.rem(c + d, cols) * reps + r
        near[k, d].wait_recv()
        s_ref[d - 1, at] = p_ref[slot, at] + a_ref[d, at]
        far[k, d] = remote(
            s_ref.at[d - 1, at], b_ref.at[d - 1, at], b_s.at[d - 1, k], b_r.at[d - 1, k], others[d - 1]
        )
        far[k, d].start()
    for k in range(pieces):
        at = pl.ds(k * size, size)
        near[k, 0].wait_recv()
        total = p_ref[me, at] + a_ref[0, at]
        for d in range(1, cols):
            far[k, d].wait_recv()
            total = total + b_ref[d - 1, at]
        out_ref[me, at] = total
        for d in range(1, cols):
            across[k, d] = remote(
                out_ref.at[me, at], out_ref.at[me, at], xs.at[d - 1, k], xr.at[d - 1, k], others[d - 1]
            )
            across[k, d].start()
        share[k] = remote(out_ref.at[me, at], out_ref.at[me, at], ps.at[k], pr.at[k], mate)
        share[k].start()
    for (k, d), copy in across.items():
        at = pl.ds(k * size, size)
        copy.wait_recv()
        slot = lax.rem(c + cols - d, cols) * reps + r
        onward[k, d] = remote(
            out_ref.at[slot, at], out_ref.at[slot, at], fs.at[d - 1, k], fr.at[d - 1, k], mate
        )
        onward[k, d].start()
    for copies in (near, far, across):
        for copy in copies.values():
            copy.wait_send()
    for copies in (share, onward):
        for copy in copies.values():
            copy.wait()


def total(parts, collective_id):
    cols, reps = lax.axis_size("col"), lax.axis_size("rep")
    if reps != 2 or cols < 2:
        return lax.psum(parts, ("col", "rep"))
    shape, kind = parts.shape[1:], parts.dtype
    pieces, _ = chunks_of(shape[0])
    dma = pltpu.SemaphoreType.DMA
    return pl.pallas_call(
        total_kernel,
        out_shape=jax.ShapeDtypeStruct(parts.shape, kind),
        in_specs=[pl.BlockSpec(memory_space=pltpu.VMEM)],
        out_specs=pl.BlockSpec(memory_space=pltpu.VMEM),
        scratch_shapes=[
            pltpu.VMEM((cols,) + shape, kind),
            pltpu.VMEM((cols - 1,) + shape, kind),
            pltpu.VMEM((cols - 1,) + shape, kind),
            dma((cols, pieces)),
            dma((cols, pieces)),
        ]
        + [dma((cols - 1, pieces))] * 6
        + [dma((pieces,))] * 2,
        compiler_params=pltpu.CompilerParams(
            collective_id=collective_id, has_side_effects=True, vmem_limit_bytes=VMEM_LIMIT
        ),
        name="total",
    )(parts)


def move_kernel(o_ref, code_ref, out_ref, arrived_ref, zs, zr, cs, cr, xs, xr, fs, fr, ps, pr, local):
    cols, reps, c, r = position()
    ntok, t = lax.axis_size("tok"), lax.axis_index("tok")
    me = c * reps + r
    mate = {"col": c, "rep": 1 - r}
    others = [{"col": lax.rem(c + d, cols), "rep": r} for d in range(1, cols)]
    peers = [{"tok": lax.rem(t + e, ntok)} for e in range(1, ntok)]
    greet([mate] + others + peers)
    along, codes, across, share, onward = [], [], {}, [], []
    for e in range(1, ntok):
        target = lax.rem(t + e, ntok)
        copy = remote(o_ref.at[target], out_ref.at[t, me], zs.at[e - 1], zr.at[e - 1], peers[e - 1])
        copy.start()
        along.append(copy)
        copy = remote(
            code_ref.at[target], arrived_ref.at[t], cs.at[e - 1], cr.at[e - 1], peers[e - 1]
        )
        copy.start()
        codes.append(copy)
    keep = pltpu.make_async_copy(o_ref.at[t], out_ref.at[t, me], local.at[0])
    keep.start()
    keep_code = pltpu.make_async_copy(code_ref.at[t], arrived_ref.at[t], local.at[1])
    keep_code.start()

    def hand_on(e):
        u = lax.rem(t + ntok - e, ntok)
        for d in range(1, cols):
            across[e, d].wait_recv()
            slot = lax.rem(c + cols - d, cols) * reps + r
            copy = remote(
                out_ref.at[u, slot], out_ref.at[u, slot], fs.at[e, d - 1], fr.at[e, d - 1], mate
            )
            copy.start()
            onward.append(copy)

    for e in range(ntok):
        u = lax.rem(t + ntok - e, ntok)
        if e:
            along[e - 1].wait_recv()
        origin = out_ref.at[u, me] if e else o_ref.at[t]
        for d in range(1, cols):
            across[e, d] = remote(
                origin, out_ref.at[u, me], xs.at[e, d - 1], xr.at[e, d - 1], others[d - 1]
            )
            across[e, d].start()
        copy = remote(origin, out_ref.at[u, me], ps.at[e], pr.at[e], mate)
        copy.start()
        share.append(copy)
        if e:
            hand_on(e - 1)
    hand_on(ntok - 1)
    keep.wait()
    keep_code.wait()
    for copy in along + list(across.values()):
        copy.wait_send()
    for copy in codes + share + onward:
        copy.wait()


def move(outgoing, codes, collective_id):
    cols, reps, ntok = lax.axis_size("col"), lax.axis_size("rep"), lax.axis_size("tok")
    if reps != 2 or cols < 2 or ntok < 2:
        incoming = lax.all_to_all(outgoing, "tok", split_axis=0, concat_axis=0, tiled=True)
        arrived = lax.all_to_all(codes, "tok", split_axis=0, concat_axis=0, tiled=True)
        return lax.all_gather(incoming, ("col", "rep"), axis=1), arrived
    dma = pltpu.SemaphoreType.DMA
    shape = (ntok, cols * reps) + outgoing.shape[1:]
    return pl.pallas_call(
        move_kernel,
        out_shape=(
            jax.ShapeDtypeStruct(shape, outgoing.dtype),
            jax.ShapeDtypeStruct(codes.shape, codes.dtype),
        ),
        in_specs=[pl.BlockSpec(memory_space=pltpu.VMEM)] * 2,
        out_specs=[pl.BlockSpec(memory_space=pltpu.VMEM)] * 2,
        scratch_shapes=[dma((ntok - 1,))] * 4
        + [dma((ntok, cols - 1))] * 4
        + [dma((ntok,))] * 2
        + [dma((2,))],
        compiler_params=pltpu.CompilerParams(
            collective_id=collective_id, has_side_effects=True, vmem_limit_bytes=VMEM_LIMIT
        ),
        name="move",
    )(outgoing, codes)


def pick_kernel(index_ref, x_ref, out_ref):
    for j in range(out_ref.shape[0]):
        out_ref[j] = x_ref[index_ref[j]]


def pick(blocks, index):
    return pl.pallas_call(
        pick_kernel,
        out_shape=jax.ShapeDtypeStruct(index.shape + blocks.shape[1:], blocks.dtype),
        in_specs=[pl.BlockSpec(memory_space=pltpu.SMEM), pl.BlockSpec(memory_space=pltpu.VMEM)],
        out_specs=pl.BlockSpec(memory_space=pltpu.VMEM),
        name="pick",
    )(index, blocks)


def attention_layer(blocks, source, layer, w_qkv, w_out, attn_gain, collective_id):
    group = blocks.shape[1]
    terms = attend(blocks, source, attn_gain[layer], w_qkv[layer], w_out[layer], group)
    rows, width = terms.shape
    return total(terms.reshape(group, rows // group, width), collective_id).reshape(rows, width)


def mlp_kernel(x_ref, gain_ref, up_ref, down_ref, share, out_ref):
    x = x_ref[...]
    hidden = dot3(split(layer_norm(x, gain_ref[...])), split(up_ref[...]))
    hidden = 0.5 * hidden * (1.0 + lax.erf(hidden * (0.5**0.5)))
    total = dot3(split(hidden), split(down_ref[...])) + x * share
    width = out_ref.shape[-1]
    for j in range(out_ref.shape[0]):
        out_ref[j] = total[:, j * width : (j + 1) * width]


def mlp_partial(stream, layer, w_up, w_down, mlp_gain, slots):
    rows, width = stream.shape
    tile = min(256, rows)
    hidden = w_up.shape[-1]
    group = lax.axis_size("col") * lax.axis_size("rep")

    def kernel(x_ref, gain_ref, up_ref, down_ref, out_ref):
        mlp_kernel(x_ref, gain_ref, up_ref, down_ref, 1.0 / group, out_ref)

    return pl.pallas_call(
        kernel,
        grid=(rows // tile,),
        in_specs=[
            pl.BlockSpec((tile, width), lambda i: (i, 0)),
            pl.BlockSpec((1, width), lambda i: (0, 0)),
            pl.BlockSpec((width, hidden), lambda i: (0, 0)),
            pl.BlockSpec((hidden, width), lambda i: (0, 0)),
        ],
        out_specs=pl.BlockSpec((slots, tile, width // slots), lambda i: (0, i, 0)),
        out_shape=jax.ShapeDtypeStruct((slots, rows, width // slots), jnp.float32),
        compiler_params=pltpu.CompilerParams(vmem_limit_bytes=48 * 1024 * 1024),
        name="mlp",
    )(stream, mlp_gain[layer][None, :], w_up[layer], w_down[layer])


def routes(dest_device, dest_slot):
    count = dest_device.shape[0]
    peers = lax.axis_size("tok")
    capacity = max(2, (count + peers - 4) // (peers - 1))
    order = jnp.arange(count, dtype=jnp.int32)
    earlier = (dest_device[:, None] == dest_device[None, :]) & (order[None, :] < order[:, None])
    place = dest_device * capacity + jnp.sum(earlier.astype(jnp.int32), axis=1)
    chosen = jnp.arange(peers * capacity, dtype=jnp.int32)[:, None] == place[None, :]
    index = jnp.sum(jnp.where(chosen, order[None, :], 0), axis=1)
    code = jnp.sum(jnp.where(chosen, dest_slot[None, :] + 1, 0), axis=1)
    code = jnp.pad(code.reshape(peers, capacity), ((0, 0), (0, 128 - capacity)))
    code = jnp.broadcast_to(code[:, None, :], (peers, 8, 128)).astype(jnp.float32)
    return index, code, capacity


def raster_cells(extended, depth_weight, point_weight, gain_row):
    row_count = extended.shape[0] - 2
    col_count = extended.shape[1] - 2
    channels = extended.shape[2]
    normed = (
        extended
        * lax.rsqrt(jnp.mean(extended * extended, axis=-1, keepdims=True) + EPSILON)
        * gain_row
    )
    mixed = jnp.zeros((row_count, col_count, channels), jnp.float32)
    for a in range(3):
        for b in range(3):
            mixed = mixed + normed[a : a + row_count, b : b + col_count] * depth_weight[a, b]
    combined = matmul(mixed.reshape(row_count * col_count, channels), point_weight)
    combined = combined.reshape(row_count, col_count, 2 * channels)
    centre = extended[1:-1, 1:-1]
    return centre + combined[..., :channels] * jax.nn.sigmoid(combined[..., channels:])


HALO = 2


def extended_cells(tok, members, rep_rows, full_width):
    cols, reps = members
    tile = []
    for col in range(cols):
        for rep in range(reps):
            y = rep * rep_rows - HALO + jnp.arange(rep_rows + 2 * HALO, dtype=jnp.int32)[:, None]
            x = col * TC - HALO + jnp.arange(TC + 2 * HALO, dtype=jnp.int32)[None, :]
            good = (y >= 0) & (y < TR) & (x >= 0) & (x < full_width)
            tile.append(jnp.where(good, (tok * TR + y) * full_width + x, -2).reshape(-1))
    return jnp.concatenate(tile)


def pool(partial, pillar, cells):
    onehot = (cells[:, None] == pillar[None, :]).astype(jnp.float32)
    return matmul(onehot, partial)


def exchange_rows(tile, ntok, reps):
    count = ntok * reps
    rep = lax.axis_index("rep")
    forward = [(i, i + 1) for i in range(count - 1)]
    backward = [(i + 1, i) for i in range(count - 1)]
    above = lax.ppermute(tile[-2 * HALO : -HALO], ("tok", "rep"), forward)
    below = lax.ppermute(tile[HALO : 2 * HALO], ("tok", "rep"), backward)
    above = jnp.where(rep == 0, above, tile[:HALO])
    below = jnp.where(rep == reps - 1, below, tile[-HALO:])
    return jnp.concatenate([above, tile[HALO:-HALO], below], axis=0)


def on_device(
    tokens,
    w_qkv,
    w_out,
    w_up,
    w_down,
    attn_gain,
    mlp_gain,
    dest_device,
    dest_slot,
    pillar,
    depth_weight,
    point_weight,
    raster_gain,
):
    members = (lax.axis_size("col"), lax.axis_size("rep"))
    group = members[0] * members[1]
    ntok = lax.axis_size("tok")
    block_count = dest_device.shape[0]
    order = jnp.arange(block_count, dtype=jnp.int32)
    index, codes, capacity = routes(dest_device, dest_slot)
    width = tokens.shape[1]
    blocks = gather(tokens, 1).reshape(1, group, block_count, -1, width)
    stream = attention_layer(blocks, order, 0, w_qkv, w_out, attn_gain, 2)
    share = scatter(mlp_partial(stream, 0, w_up, w_down, mlp_gain, group), 3)
    outgoing = pick(share.reshape(block_count, -1, width), index)
    outgoing = outgoing.reshape(ntok, -1, width)
    moved, arrived = move(outgoing, codes, 4)
    blocks = moved.reshape(ntok, group, capacity, -1, width)
    held = arrived[:, 0, :capacity].reshape(-1).astype(jnp.int32)
    found = held[None, :] == order[:, None] + 1
    source = jnp.sum(jnp.where(found, jnp.arange(held.shape[0], dtype=jnp.int32)[None, :], 0), axis=1)
    stream = attention_layer(blocks, source, 1, w_qkv, w_out, attn_gain, 5)
    partial = mlp_partial(stream, 1, w_up, w_down, mlp_gain, 1)[0]

    rep_rows = TR // members[1]
    full_width = TC * members[0]
    cells = extended_cells(lax.axis_index("tok"), members, rep_rows, full_width)
    pooled = pool(partial, pillar, cells)
    parts = pooled.reshape(group, -1, pooled.shape[1])
    edge = HALO * (TC + 2 * HALO)
    inside_kernel = members[0] > 1 and members[1] == 2 and ntok > 1 and edge % 8 == 0
    tile = scatter(parts, 6, edge if inside_kernel else 0)
    tile = tile.reshape(rep_rows + 2 * HALO, TC + 2 * HALO, -1)
    if not inside_kernel:
        tile = exchange_rows(tile, ntok, members[1])
    first = raster_cells(tile, depth_weight[0], point_weight[0], raster_gain[0])
    y = lax.axis_index(("tok", "rep")) * rep_rows - 1 + jnp.arange(rep_rows + 2)[:, None, None]
    x = lax.axis_index("col") * TC - 1 + jnp.arange(TC + 2)[None, :, None]
    inside = (y >= 0) & (y < TR * ntok) & (x >= 0) & (x < full_width)
    first = jnp.where(inside, first, 0.0)
    return raster_cells(first, depth_weight[1], point_weight[1], raster_gain[1])


def solution(mesh):
    placed = (
        P(("scene", "tok"), ("col", "rep")),
        P(None, None, None, ("col", "rep")),
        P(None, ("col", "rep"), None),
        P(None, None, ("col", "rep")),
        P(None, ("col", "rep"), None),
        P(),
        P(),
        P(("scene", "tok")),
        P(("scene", "tok")),
        P(("scene", "tok")),
        P(),
        P(),
        P(),
    )
    return jax.shard_map(
        on_device,
        mesh=mesh,
        in_specs=placed,
        out_specs=P(("scene", "tok", "rep"), "col", None),
        check_vma=False,
    )
```
